32 devices in a mesh: row: 8 (over y, x, core), col: 4 (over z).
Axes of the slice: x: 2, y: 2, z: 4, core: 2. Of those that a mesh axis runs over, the one named last changes fastest.
Arguments:
- probes: float32 [16384, 256], P(('row', 'col')), may hold values from -6 to 6
- spectrum: float32 [32, 512], P(('row', 'col')), may hold values from 0.5 to 4
Outputs:
- leaf_basis: float32 [16384, 256], P(('row', 'col'))
- leaf_transfer: float32 [8192, 256], P(('row', 'col'))
- pair_transfer: float32 [4096, 256], P(('row', 'col'))
- group_factor: float32 [2048, 256], P(('row', 'col'))
The draws below stay inside these ranges and needn't reach their ends.
All inputs are finite; a program needn't handle non-finite values.
Results may differ from the reference program's by a relative error of at most 0.000076.
Values sent between devices are 32-bit elements; how exact they have to be, the bound alone decides.
No kernel may reach another device: no remote copies, remote signals or barrier semaphores. Data moves between devices by JAX's collectives and lax.ppermute only.
A program may use at most 64 MiB of HBM per device.

```python
import math
import jax
import jax.numpy as jnp
from jax import lax

M = 512
R = 256
N = 16384
N_ROW = 8
N_COL = 4


def steps_of(stream_key, shape, split, least, high):
    gain, own = 1.0, jax.random.fold_in(stream_key, 6)
    for dim, blocks in split:
        heights = jnp.exp(jax.random.uniform(jax.random.fold_in(own, dim), (blocks,), jnp.float32, least / len(split), high / len(split)))
        gain = gain * jnp.repeat(heights, shape[dim] // blocks).reshape([-1 if axis == dim else 1 for axis in range(len(shape))])
    return gain


def normal_values(stream_key, extent, spread, limit, split=(), held_as=jnp.bfloat16):
    gain = steps_of(stream_key, extent, split, -0.22, 0.18) if split else 1.0
    array = jax.random.normal(stream_key, extent, jnp.float32) * spread * gain
    return jnp.minimum(jnp.maximum(array, -limit), limit).astype(held_as)


def setup_inputs(seed: int = 0) -> dict:
    arg_keys = jax.random.split(jax.random.key(seed), 3)
    probes = normal_values(arg_keys[0], (N, R), 1.0, 6.0, ((0, 32),), jnp.float32)
    spectrum = jnp.clip(jnp.exp(math.log(4.0) - 2.0794415 * jax.random.uniform(arg_keys[1], (N_ROW * N_COL, M), jnp.float32) ** steps_of(arg_keys[1], (N_ROW * N_COL, M), ((0, 32),), -0.2, 0.2)), 0.5, 4.0)
    return {"probes": probes, "spectrum": spectrum}


def lower_solve(low, rhs):
    return jax.scipy.linalg.solve_triangular(low, rhs, lower=True)

def reference(probes, spectrum):
    devices = spectrum.shape[0]
    rows_dev = spectrum.shape[1]
    width = probes.shape[1]
    symbol = spectrum.T.reshape(-1)
    spectra = jnp.fft.fft(probes, axis=0)
    sample = jnp.real(jnp.fft.ifft(spectra * symbol[:, None], axis=0)).astype(jnp.float32)
    blocks = sample.reshape(devices, rows_dev, width)
    leaf_gram = jnp.einsum('pmr,pms->prs', blocks, blocks, precision=lax.Precision.HIGHEST) / rows_dev
    leaf_low = jnp.linalg.cholesky(leaf_gram)
    leaf_basis = jax.vmap(lambda low, block: lower_solve(low, block.T).T)(leaf_low, blocks)
    pair_gram = leaf_gram[0::2] + leaf_gram[1::2]
    pair_low = jnp.linalg.cholesky(pair_gram)
    pair_rep = jnp.repeat(pair_low, 2, axis=0)
    leaf_transfer = jnp.swapaxes(jax.vmap(lower_solve)(pair_rep, leaf_low), 1, 2)
    group_gram = pair_gram[0::2] + pair_gram[1::2]
    group_low = jnp.linalg.cholesky(group_gram)
    group_rep = jnp.repeat(group_low, 2, axis=0)
    pair_transfer = jnp.swapaxes(jax.vmap(lower_solve)(group_rep, pair_low), 1, 2)
    group_factor = jnp.swapaxes(group_low, 1, 2)
    return (leaf_basis.reshape(devices * rows_dev, width), leaf_transfer.reshape(devices * width, width), pair_transfer.reshape(devices * width // 2, width), group_factor.reshape(devices * width // 4, width))
```

```python
import math

import jax
import jax.numpy as jnp
import numpy as np
from jax import lax
from jax.experimental import pallas as pl
from jax.experimental.pallas import tpu as pltpu
from jax.sharding import PartitionSpec as P

LANES = 128
HIGHEST = lax.Precision.HIGHEST


def partner(value, axis, distance):
    mask = 2**distance
    pairs = [(source, source ^ mask) for source in range(lax.axis_size(axis))]
    return lax.ppermute(value, axis, pairs)


def matmul(left, right):
    return jnp.dot(left, right, precision=HIGHEST, preferred_element_type=jnp.float32)


def circle(product, length):
    angle = 2.0 * np.pi / length * (product % length)
    return np.cos(angle), np.sin(angle)


def tables(devices, split):
    major = devices * split
    total = major * LANES
    order = (np.arange(devices)[None, :] * split + np.arange(split)[:, None]).reshape(-1)
    freq = np.arange(major)
    cos, sin = circle(freq[:, None] * order[None, :], major)
    first = np.block([[cos, sin], [-sin, cos]])
    lane = np.arange(LANES)
    cos, sin = circle(lane[:, None] * lane[None, :], LANES)
    second = np.block([[cos, -sin], [sin, cos]])
    cos_turn, sin_turn = circle(freq[:, None] * lane[None, :], total)
    turn = np.stack([cos_turn, sin_turn])
    return [np.asarray(t, np.float32) for t in (first, first.T, second, second.T, turn)]


def circulant_kernel(devices, split, per_dev):
    major = devices * split
    pairs = per_dev // 2

    width = devices * per_dev

    def body(
        x_ref, lam_ref, first_ref, first_t_ref, second_ref, second_t_ref, turn_ref, o_ref, tile_ref
    ):
        cos = turn_ref[0]
        sin = turn_ref[1]
        for j in range(split):
            tile_ref[j * width : (j + 1) * width, :] = x_ref[:, j * LANES : (j + 1) * LANES]

        def column(c):
            return [
                tile_ref[pl.ds(j * width + c, devices, stride=per_dev), :] for j in range(split)
            ]

        packed = jnp.concatenate(
            [jnp.concatenate(column(2 * q) + column(2 * q + 1), 0) for q in range(pairs)], 1
        )
        mixed = matmul(first_ref[...], packed)
        turned = []
        for q in range(pairs):
            real = mixed[:major, q * LANES : (q + 1) * LANES]
            imag = mixed[major:, q * LANES : (q + 1) * LANES]
            turned.append(
                jnp.concatenate([real * cos + imag * sin, imag * cos - real * sin], 1)
            )
        spectra = matmul(jnp.concatenate(turned, 0), second_ref[...])
        lam = lam_ref[...]
        lam = jnp.concatenate([lam, lam], 1)
        spectra = jnp.concatenate(
            [spectra[q * major : (q + 1) * major] * lam for q in range(pairs)], 0
        )
        back = matmul(spectra, second_t_ref[...])
        turned = []
        for q in range(pairs):
            real = back[q * major : (q + 1) * major, :LANES]
            imag = back[q * major : (q + 1) * major, LANES:]
            turned.append(
                jnp.concatenate([real * cos - imag * sin, imag * cos + real * sin], 0)
            )
        sample = matmul(first_t_ref[...], jnp.concatenate(turned, 1))
        for c in range(per_dev):
            for j in range(split):
                row = (c % 2) * major + j * devices
                lane = (c // 2) * LANES
                tile_ref[pl.ds(j * width + c, devices, stride=per_dev), :] = sample[
                    row : row + devices, lane : lane + LANES
                ]
        for j in range(split):
            o_ref[:, j * LANES : (j + 1) * LANES] = tile_ref[j * width : (j + 1) * width, :]

    return body


def circulant(columns, lam, devices):
    width, rows_dev = columns.shape
    split = rows_dev // LANES
    return pl.pallas_call(
        circulant_kernel(devices, split, width // devices),
        out_shape=jax.ShapeDtypeStruct(columns.shape, jnp.float32),
        scratch_shapes=[pltpu.VMEM((split * width, LANES), jnp.float32)],
        compiler_params=pltpu.CompilerParams(vmem_limit_bytes=48 << 20),
        name="circulant",
    )(columns, lam, *tables(devices, split))


def symmetric_symbol(spectrum, devices):
    split = spectrum.shape[1] // LANES
    major = devices * split
    own = jnp.broadcast_to(spectrum.reshape(LANES, split).T[None], (devices, split, LANES))
    every = lax.all_to_all(own, ("row", "col"), split_axis=0, concat_axis=0, tiled=True)
    lam = every.swapaxes(0, 1).reshape(major, LANES)
    head = lam[:1]
    head = jnp.concatenate([head[:, :1], jnp.flip(head[:, 1:], 1)], 1)
    back = jnp.concatenate([head, jnp.flip(lam[1:], (0, 1))], 0)
    return (lam + back) * (0.5 / (major * LANES))


def factor_kernel(problems, width, block):
    tiles = width // LANES

    def body(gram_ref, upper_ref, inverse_ref, tile_ref):
        row = lax.broadcasted_iota(jnp.int32, (width, LANES), 0)
        lane = lax.broadcasted_iota(jnp.int32, (width, LANES), 1)
        for t in range(tiles):
            unit = jnp.where(row == lane + t * LANES, 1.0, 0.0).astype(jnp.float32)
            for p in range(problems):
                rows = slice(p * width, (p + 1) * width)
                tile_ref[t, rows, :] = gram_ref[p, :, t * LANES : (t + 1) * LANES]
                tile_ref[tiles + t, rows, :] = unit
        for base in range(0, width, block):
            own = base // LANES
            offset = base % LANES
            active = list(range(own, tiles)) + list(range(tiles, tiles + own + 1))
            panel = [
                [tile_ref[t, pl.ds(base + i, problems, stride=width), :] for t in active]
                for i in range(block)
            ]
            entry = {
                (i, j): jnp.broadcast_to(
                    panel[i][0][:, offset + j : offset + j + 1], (problems, LANES)
                )
                for i in range(block)
                for j in range(i, block)
            }
            for j in range(block):
                scale = lax.rsqrt(entry[j, j])
                factor = {i: entry[j, i] * scale for i in range(j + 1, block)}
                panel[j] = [x * scale for x in panel[j]]
                for i in range(j + 1, block):
                    for l in range(i, block):
                        entry[i, l] = entry[i, l] - factor[i] * factor[l]
                    panel[i] = [x - factor[i] * y for x, y in zip(panel[i], panel[j])]
                for x, t in zip(panel[j], active):
                    tile_ref[t, pl.ds(base + j, problems, stride=width), :] = x
            after = base + block
            if after < width:
                for p in range(problems):
                    done = jnp.concatenate(
                        [tile_ref[t, p * width + base : p * width + after, :] for t in active], 1
                    )
                    update = lax.dot_general(
                        done[:, : (tiles - own) * LANES],
                        done,
                        (((0,), (0,)), ((), ())),
                        precision=HIGHEST,
                        preferred_element_type=jnp.float32,
                    )
                    rows = slice(p * width + after, (p + 1) * width)
                    for q, t in enumerate(active):
                        tile_ref[t, rows, :] = (
                            tile_ref[t, rows, :]
                            - update[after - own * LANES :, q * LANES : (q + 1) * LANES]
                        )
        for t in range(tiles):
            lanes = slice(t * LANES, (t + 1) * LANES)
            for p in range(problems):
                rows = slice(p * width, (p + 1) * width)
                upper_ref[p, :, lanes] = jnp.where(
                    lane + t * LANES >= row, tile_ref[t, rows, :], 0.0
                )
                inverse_ref[p, :, lanes] = jnp.where(
                    lane + t * LANES <= row, tile_ref[tiles + t, rows, :], 0.0
                )

    return body


def factor(grams):
    problems, width, _ = grams.shape
    return pl.pallas_call(
        factor_kernel(problems, width, 16),
        out_shape=[jax.ShapeDtypeStruct(grams.shape, jnp.float32)] * 2,
        scratch_shapes=[pltpu.VMEM((2 * width // LANES, problems * width, LANES), jnp.float32)],
        compiler_params=pltpu.CompilerParams(vmem_limit_bytes=48 << 20),
        name="factor",
    )(grams)


def local(probes, spectrum):
    rows_dev, width = probes.shape
    devices = lax.axis_size("row") * lax.axis_size("col")
    col_index = lax.axis_index("col")
    axes = ("row", "col")
    lam = symmetric_symbol(spectrum, devices)
    columns = lax.all_to_all(probes.T, axes, split_axis=0, concat_axis=0, tiled=True)
    moved = circulant(columns, lam, devices)
    sample_t = lax.all_to_all(moved, axes, split_axis=0, concat_axis=0, tiled=True)
    leaf_gram = matmul(sample_t, sample_t.T) / rows_dev
    pair_gram = leaf_gram + partner(leaf_gram, "col", 0)
    group_gram = pair_gram + partner(pair_gram, "col", 1)
    upper, inverse = factor(jnp.stack([leaf_gram, pair_gram, group_gram]))
    half = width // 2
    quarter = width // 4
    pair_upper = lax.dynamic_slice_in_dim(upper[1], col_index % 2 * half, half, 0)
    group_factor = lax.dynamic_slice_in_dim(upper[2], col_index % 4 * quarter, quarter, 0)
    leaf_basis = matmul(sample_t.T, inverse[0].T)
    leaf_transfer = matmul(upper[0], inverse[1].T)
    pair_transfer = matmul(pair_upper, inverse[2].T)
    return (leaf_basis, leaf_transfer, pair_transfer, group_factor)


def solution(mesh):
    placed = P(("row", "col"), None)
    return jax.shard_map(
        local,
        mesh=mesh,
        in_specs=(placed, placed),
        out_specs=(placed, placed, placed, placed),
        check_vma=False,
    )
```

```python
import math

import jax
import jax.numpy as jnp
import numpy as np
from jax import lax
from jax.experimental import pallas as pl
from jax.experimental.pallas import tpu as pltpu
from jax.sharding import PartitionSpec as P

LANES = 128
HIGHEST = lax.Precision.HIGHEST


def partner(value, axis, distance):
    mask = 2**distance
    pairs = [(source, source ^ mask) for source in range(lax.axis_size(axis))]
    return lax.ppermute(value, axis, pairs)


def matmul(left, right):
    return jnp.dot(left, right, precision=HIGHEST, preferred_element_type=jnp.float32)


def circle(product, length):
    angle = 2.0 * np.pi / length * (product % length)
    return np.cos(angle), np.sin(angle)


def tables(devices, split):
    major = devices * split
    total = major * LANES
    order = (np.arange(devices)[None, :] * split + np.arange(split)[:, None]).reshape(-1)
    freq = np.arange(major)
    cos, sin = circle(freq[:, None] * order[None, :], major)
    first = np.block([[cos, sin], [-sin, cos]])
    lane = np.arange(LANES)
    cos, sin = circle(lane[:, None] * lane[None, :], LANES)
    second = np.block([[cos, -sin], [sin, cos]])
    cos_turn, sin_turn = circle(freq[:, None] * lane[None, :], total)
    turn = np.stack([cos_turn, sin_turn])
    return [np.asarray(t, np.float32) for t in (first, first.T, second, second.T, turn)]


def circulant_kernel(devices, split, per_dev):
    major = devices * split
    pairs = per_dev // 2

    width = devices * per_dev

    def body(
        x_ref, lam_ref, first_ref, first_t_ref, second_ref, second_t_ref, turn_ref, o_ref, tile_ref
    ):
        cos = turn_ref[0]
        sin = turn_ref[1]
        for j in range(split):
            tile_ref[j * width : (j + 1) * width, :] = x_ref[:, j * LANES : (j + 1) * LANES]

        def column(c):
            return [
                tile_ref[pl.ds(j * width + c, devices, stride=per_dev), :] for j in range(split)
            ]

        packed = jnp.concatenate(
            [jnp.concatenate(column(2 * q) + column(2 * q + 1), 0) for q in range(pairs)], 1
        )
        mixed = matmul(first_ref[...], packed)
        turned = []
        for q in range(pairs):
            real = mixed[:major, q * LANES : (q + 1) * LANES]
            imag = mixed[major:, q * LANES : (q + 1) * LANES]
            turned.append(
                jnp.concatenate([real * cos + imag * sin, imag * cos - real * sin], 1)
            )
        spectra = matmul(jnp.concatenate(turned, 0), second_ref[...])
        lam = lam_ref[...]
        lam = jnp.concatenate([lam, lam], 1)
        spectra = jnp.concatenate(
            [spectra[q * major : (q + 1) * major] * lam for q in range(pairs)], 0
        )
        back = matmul(spectra, second_t_ref[...])
        turned = []
        for q in range(pairs):
            real = back[q * major : (q + 1) * major, :LANES]
            imag = back[q * major : (q + 1) * major, LANES:]
            turned.append(
                jnp.concatenate([real * cos - imag * sin, imag * cos + real * sin], 0)
            )
        sample = matmul(first_t_ref[...], jnp.concatenate(turned, 1))
        for c in range(per_dev):
            for j in range(split):
                row = (c % 2) * major + j * devices
                lane = (c // 2) * LANES
                tile_ref[pl.ds(j * width + c, devices, stride=per_dev), :] = sample[
                    row : row + devices, lane : lane + LANES
                ]
        for j in range(split):
            o_ref[:, j * LANES : (j + 1) * LANES] = tile_ref[j * width : (j + 1) * width, :]

    return body


def circulant(columns, lam, devices):
    width, rows_dev = columns.shape
    split = rows_dev // LANES
    return pl.pallas_call(
        circulant_kernel(devices, split, width // devices),
        out_shape=jax.ShapeDtypeStruct(columns.shape, jnp.float32),
        scratch_shapes=[pltpu.VMEM((split * width, LANES), jnp.float32)],
        compiler_params=pltpu.CompilerParams(vmem_limit_bytes=48 << 20),
        name="circulant",
    )(columns, lam, *tables(devices, split))


def symmetric_symbol(every, devices):
    split = every.shape[1] // LANES
    major = devices * split
    lam = every.reshape(devices, LANES, split).transpose(2, 0, 1).reshape(major, LANES)
    head = lam[:1]
    head = jnp.concatenate([head[:, :1], jnp.flip(head[:, 1:], 1)], 1)
    back = jnp.concatenate([head, jnp.flip(lam[1:], (0, 1))], 0)
    return (lam + back) * (0.5 / (major * LANES))


def iota(shape, dim):
    return lax.broadcasted_iota(jnp.int32, shape, dim)


def times_transpose(left, right):
    return lax.dot_general(
        left,
        right,
        (((1,), (1,)), ((), ())),
        precision=HIGHEST,
        preferred_element_type=jnp.float32,
    )


def gram_kernel(sample_ref, packed_ref):
    width, rows = sample_ref.shape
    upper = times_transpose(sample_ref[:LANES, :], sample_ref[...]) * (1.0 / rows)
    last = sample_ref[LANES:, :]
    last = times_transpose(last, last) * (1.0 / rows)
    row = iota((LANES, LANES), 0)
    lane = iota((LANES, LANES), 1)
    packed_ref[:LANES, :] = jnp.where(lane >= row, upper[:, :LANES], last)
    packed_ref[LANES : 2 * LANES, :] = upper[:, LANES:]
    diagonal = jnp.sum(jnp.where(lane == row, last, 0.0), axis=0, keepdims=True)
    packed_ref[2 * LANES :, :] = jnp.broadcast_to(diagonal, (8, LANES))


def packed_gram(sample_t):
    return pl.pallas_call(
        gram_kernel,
        out_shape=jax.ShapeDtypeStruct((2 * LANES + 8, LANES), jnp.float32),
        name="gram",
    )(sample_t)


def parts(value):
    high = value.astype(jnp.bfloat16).astype(jnp.float32)
    rest = value - high
    middle = rest.astype(jnp.bfloat16).astype(jnp.float32)
    return high, middle, rest - middle


def eliminate(tile_ref, problems, width, block):
    tiles = width // LANES
    thin = iota((problems, LANES), 1)
    for base in range(0, width, block):
        own = base // LANES
        offset = base % LANES
        order = [own] + [t for t in range(tiles) if t != own]
        panel = [
            [tile_ref[t, pl.ds(base + i, problems, stride=width), :] for t in order]
            for i in range(block)
        ]
        entry = {
            (i, j): jnp.broadcast_to(
                panel[i][0][:, offset + j : offset + j + 1], (problems, LANES)
            )
            for i in range(block)
            for j in range(i, block)
        }
        for j in range(block):
            scale = lax.rsqrt(entry[j, j])
            factor = {i: entry[j, i] * scale for i in range(j + 1, block)}
            hot = thin == offset + j
            panel[j] = [jnp.where(hot, 1.0, panel[j][0]) * scale] + [
                x * scale for x in panel[j][1:]
            ]
            for i in range(j + 1, block):
                for l in range(i, block):
                    entry[i, l] = entry[i, l] - factor[i] * factor[l]
                kept = [jnp.where(hot, 0.0, panel[i][0])] + panel[i][1:]
                panel[i] = [x - factor[i] * y for x, y in zip(kept, panel[j])]
            for x, t in zip(panel[j], order):
                tile_ref[t, pl.ds(base + j, problems, stride=width), :] = x
        after = base + block
        if after == width:
            continue
        first = after // LANES * LANES
        lane = iota((block, LANES), 1) - offset
        inverse = (lane < 0) | (lane >= block) | (lane <= iota((block, LANES), 0))
        below = iota((width - after, LANES), 1) - offset
        below = (below >= 0) & (below < block)
        for p in range(problems):
            start = p * width
            rows = [parts(tile_ref[t, start + base : start + after, :]) for t in range(tiles)]
            left = jnp.concatenate(
                [
                    jnp.concatenate([rows[t][q] for q in (0, 0, 1, 1, 0, 2)], 0)
                    for t in range(first // LANES, tiles)
                ],
                1,
            ).astype(jnp.bfloat16)
            rows[own] = [jnp.where(inverse, x, 0.0) for x in rows[own]]
            right = jnp.concatenate(
                [
                    jnp.concatenate([rows[t][q] for q in (0, 1, 0, 1, 2, 0)], 0)
                    for t in range(tiles)
                ],
                1,
            ).astype(jnp.bfloat16)
            update = lax.dot_general(
                left, right, (((0,), (0,)), ((), ())), preferred_element_type=jnp.float32
            )
            for t in range(tiles):
                old = tile_ref[t, start + after : start + width, :]
                if t == own:
                    old = jnp.where(below, 0.0, old)
                tile_ref[t, start + after : start + width, :] = (
                    old - update[after - first :, t * LANES : (t + 1) * LANES]
                )


def finish_kernel(
    place_ref,
    sample_ref,
    leaf_ref,
    pair_ref,
    group_ref,
    basis_ref,
    leaf_transfer_ref,
    pair_transfer_ref,
    group_factor_ref,
    tile_ref,
    upper_ref,
):
    width = sample_ref.shape[0]
    row = iota((LANES, LANES), 0)
    lane = iota((LANES, LANES), 1)
    for p, packed_ref in enumerate((leaf_ref, pair_ref, group_ref)):
        start = p * width
        shared = packed_ref[:LANES, :]
        tile_ref[0, start : start + LANES, :] = shared
        tile_ref[0, start + LANES : start + width, :] = jnp.zeros((LANES, LANES), jnp.float32)
        tile_ref[1, start : start + LANES, :] = packed_ref[LANES : 2 * LANES, :]
        diagonal = jnp.broadcast_to(packed_ref[2 * LANES : 2 * LANES + 1, :], (LANES, LANES))
        tile_ref[1, start + LANES : start + width, :] = jnp.where(
            lane == row, diagonal, shared.T
        )
    eliminate(tile_ref, 3, width, 16)
    row = iota((width, width), 0)
    lane = iota((width, width), 1)
    inverse = []
    for p in range(3):
        start = p * width
        whole = jnp.concatenate([tile_ref[t, start : start + width, :] for t in range(2)], 1)
        inverse.append(jnp.where(lane <= row, whole, 0.0))
        upper_ref[p] = jnp.where(
            lane > row, whole, jnp.where(lane == row, 1.0 / whole, 0.0)
        )
    basis_ref[...] = times_transpose(sample_ref[...].T, inverse[0])
    leaf_transfer_ref[...] = times_transpose(upper_ref[0], inverse[1])
    half = width // 2
    quarter = width // 4
    place = place_ref[0]
    pair_upper = upper_ref[1, pl.ds(pl.multiple_of(place % 2 * half, half), half), :]
    pair_transfer_ref[...] = times_transpose(pair_upper, inverse[2])
    group_factor_ref[...] = upper_ref[
        2, pl.ds(pl.multiple_of(place % 4 * quarter, quarter), quarter), :
    ]


def finish(place, sample_t, leaf, pair, group):
    width, rows = sample_t.shape
    shapes = [(rows, width), (width, width), (width // 2, width), (width // 4, width)]
    return pl.pallas_call(
        finish_kernel,
        out_shape=[jax.ShapeDtypeStruct(shape, jnp.float32) for shape in shapes],
        in_specs=[pl.BlockSpec(memory_space=pltpu.SMEM)]
        + [pl.BlockSpec(memory_space=pltpu.VMEM)] * 4,
        scratch_shapes=[
            pltpu.VMEM((width // LANES, 3 * width, LANES), jnp.float32),
            pltpu.VMEM((3, width, width), jnp.float32),
        ],
        compiler_params=pltpu.CompilerParams(vmem_limit_bytes=48 << 20),
        name="finish",
    )(place, sample_t, leaf, pair, group)


def local(probes, spectrum):
    devices = lax.axis_size("row") * lax.axis_size("col")
    axes = ("row", "col")
    turned, spectrum = lax.optimization_barrier((probes.T, spectrum))
    columns = lax.all_to_all(turned, axes, split_axis=0, concat_axis=0, tiled=True)
    every = lax.all_to_all(
        jnp.broadcast_to(spectrum, (devices, spectrum.shape[1])),
        axes,
        split_axis=0,
        concat_axis=0,
        tiled=True,
    )
    moved = circulant(columns, symmetric_symbol(every, devices), devices)
    sample_t = lax.all_to_all(moved, axes, split_axis=0, concat_axis=0, tiled=True)
    leaf = packed_gram(sample_t)
    pair = leaf + partner(leaf, "col", 0)
    group = pair + partner(pair, "col", 1)
    place = lax.axis_index("col").reshape(1).astype(jnp.int32)
    return tuple(finish(place, sample_t, leaf, pair, group))


def solution(mesh):
    placed = P(("row", "col"), None)
    return jax.shard_map(
        local,
        mesh=mesh,
        in_specs=(placed, placed),
        out_specs=(placed, placed, placed, placed),
        check_vma=False,
    )
```

```python
import math

import jax
import jax.numpy as jnp
import numpy as np
from jax import lax
from jax.experimental import pallas as pl
from jax.experimental.pallas import tpu as pltpu
from jax.sharding import PartitionSpec as P

LANES = 128
HIGHEST = lax.Precision.HIGHEST


def partner(value, axis, distance):
    mask = 2**distance
    pairs = [(source, source ^ mask) for source in range(lax.axis_size(axis))]
    return lax.ppermute(value, axis, pairs)


def matmul(left, right):
    return jnp.dot(left, right, precision=HIGHEST, preferred_element_type=jnp.float32)


def circle(product, length):
    angle = 2.0 * np.pi / length * (product % length)
    return np.cos(angle), np.sin(angle)


def tables(devices, split):
    major = devices * split
    total = major * LANES
    order = (np.arange(devices)[None, :] * split + np.arange(split)[:, None]).reshape(-1)
    freq = np.arange(major)
    cos, sin = circle(freq[:, None] * order[None, :], major)
    first = np.block([[cos, sin], [-sin, cos]])
    lane = np.arange(LANES)
    cos, sin = circle(lane[:, None] * lane[None, :], LANES)
    second = np.block([[cos, -sin], [sin, cos]])
    cos_turn, sin_turn = circle(freq[:, None] * lane[None, :], total)
    turn = np.stack([cos_turn, sin_turn])
    return [np.asarray(t, np.float32) for t in (first, first.T, second, second.T, turn)]


def iota(shape, dim):
    return lax.broadcasted_iota(jnp.int32, shape, dim)


def times_transpose(left, right):
    return lax.dot_general(
        left,
        right,
        (((1,), (1,)), ((), ())),
        precision=HIGHEST,
        preferred_element_type=jnp.float32,
    )


def spread_kernel(per_dev, extra):
    def body(probes_ref, spectrum_ref, o_ref):
        rows, width = probes_ref.shape
        split = rows // LANES
        for j in range(split):
            lanes = slice(j * LANES, (j + 1) * LANES)
            o_ref[:, lanes] = probes_ref[lanes, :].T
        place = iota((LANES, rows), 1)
        own = jnp.where(place // split == iota((LANES, rows), 0), spectrum_ref[...], 0.0)
        for t in range(extra):
            part = iota((8, rows), 0) % per_dev + t * per_dev
            pick = jnp.where(iota((8, rows), 1) % split == part, 1.0, 0.0)
            symbol = times_transpose(pick, own)
            for r in range(0, width, 8):
                o_ref[r : r + 8, rows + t * LANES : rows + (t + 1) * LANES] = symbol

    return body


def spread(probes, spectrum, devices):
    rows, width = probes.shape
    per_dev = width // devices
    extra = pl.cdiv(rows // LANES, per_dev)
    return pl.pallas_call(
        spread_kernel(per_dev, extra),
        out_shape=jax.ShapeDtypeStruct((width, rows + extra * LANES), jnp.float32),
        name="spread",
    )(probes, spectrum)


def circulant_kernel(devices, split, per_dev, extra):
    major = devices * split
    pairs = per_dev // 2
    width = devices * per_dev

    def symmetric_symbol(tile_ref):
        lam = jnp.concatenate(
            [
                tile_ref[
                    pl.ds((split + h // per_dev) * width + h % per_dev, devices, stride=per_dev), :
                ]
                for h in range(split)
            ],
            0,
        )
        row = iota((LANES, LANES), 0)
        lane = iota((LANES, LANES), 1)
        flip = jnp.where(row + lane == LANES - 1, 1.0, 0.0)
        head_flip = jnp.where((row + lane) % LANES == 0, 1.0, 0.0)
        back = matmul(lam, jnp.concatenate([flip, head_flip], 1))
        row = iota((major, major), 0)
        lane = iota((major, major), 1)
        turn = jnp.where(row + lane == major, 1.0, 0.0)
        other = jnp.where(
            iota((major, LANES), 0) == 0, back[:, LANES:], matmul(turn, back[:, :LANES])
        )
        return (lam + other) * (0.5 / (major * LANES))

    def body(x_ref, first_ref, first_t_ref, second_ref, second_t_ref, turn_ref, o_ref, tile_ref):
        cos = turn_ref[0]
        sin = turn_ref[1]
        for j in range(split + extra):
            tile_ref[j * width : (j + 1) * width, :] = x_ref[:, j * LANES : (j + 1) * LANES]
        lam = symmetric_symbol(tile_ref)

        def column(c):
            return [
                tile_ref[pl.ds(j * width + c, devices, stride=per_dev), :] for j in range(split)
            ]

        packed = jnp.concatenate(
            [jnp.concatenate(column(2 * q) + column(2 * q + 1), 0) for q in range(pairs)], 1
        )
        mixed = matmul(first_ref[...], packed)
        turned = []
        for q in range(pairs):
            real = mixed[:major, q * LANES : (q + 1) * LANES]
            imag = mixed[major:, q * LANES : (q + 1) * LANES]
            turned.append(
                jnp.concatenate([real * cos + imag * sin, imag * cos - real * sin], 1)
            )
        spectra = matmul(jnp.concatenate(turned, 0), second_ref[...])
        lam = jnp.concatenate([lam, lam], 1)
        spectra = jnp.concatenate(
            [spectra[q * major : (q + 1) * major] * lam for q in range(pairs)], 0
        )
        back = matmul(spectra, second_t_ref[...])
        turned = []
        for q in range(pairs):
            real = back[q * major : (q + 1) * major, :LANES]
            imag = back[q * major : (q + 1) * major, LANES:]
            turned.append(
                jnp.concatenate([real * cos - imag * sin, imag * cos + real * sin], 0)
            )
        sample = matmul(first_t_ref[...], jnp.concatenate(turned, 1))
        for c in range(per_dev):
            for j in range(split):
                row = (c % 2) * major + j * devices
                lane = (c // 2) * LANES
                tile_ref[pl.ds(j * width + c, devices, stride=per_dev), :] = sample[
                    row : row + devices, lane : lane + LANES
                ]
        for j in range(split):
            o_ref[:, j * LANES : (j + 1) * LANES] = tile_ref[j * width : (j + 1) * width, :]

    return body


def circulant(columns, rows, devices):
    width = columns.shape[0]
    split = rows // LANES
    tiles = columns.shape[1] // LANES
    return pl.pallas_call(
        circulant_kernel(devices, split, width // devices, tiles - split),
        out_shape=jax.ShapeDtypeStruct((width, rows), jnp.float32),
        scratch_shapes=[pltpu.VMEM((tiles * width, LANES), jnp.float32)],
        compiler_params=pltpu.CompilerParams(vmem_limit_bytes=48 << 20),
        name="circulant",
    )(columns, *tables(devices, split))


def gram_kernel(sample_ref, packed_ref):
    width, rows = sample_ref.shape
    upper = times_transpose(sample_ref[:LANES, :], sample_ref[...]) * (1.0 / rows)
    last = sample_ref[LANES:, :]
    last = times_transpose(last, last) * (1.0 / rows)
    row = iota((LANES, LANES), 0)
    lane = iota((LANES, LANES), 1)
    packed_ref[:LANES, :] = jnp.where(lane >= row, upper[:, :LANES], last)
    packed_ref[LANES : 2 * LANES, :] = upper[:, LANES:]
    diagonal = jnp.sum(jnp.where(lane == row, last, 0.0), axis=0, keepdims=True)
    packed_ref[2 * LANES :, :] = jnp.broadcast_to(diagonal, (8, LANES))


def packed_gram(sample_t):
    return pl.pallas_call(
        gram_kernel,
        out_shape=jax.ShapeDtypeStruct((2 * LANES + 8, LANES), jnp.float32),
        name="gram",
    )(sample_t)


def parts(value):
    high = value.astype(jnp.bfloat16).astype(jnp.float32)
    rest = value - high
    middle = rest.astype(jnp.bfloat16).astype(jnp.float32)
    return high, middle, rest - middle


def eliminate(tile_ref, problems, width, block):
    tiles = width // LANES
    thin = iota((problems, LANES), 1)
    for base in range(0, width, block):
        own = base // LANES
        offset = base % LANES
        order = [own] + [t for t in range(tiles) if t != own]
        panel = [
            [tile_ref[t, pl.ds(base + i, problems, stride=width), :] for t in order]
            for i in range(block)
        ]
        entry = {
            (i, j): jnp.broadcast_to(
                panel[i][0][:, offset + j : offset + j + 1], (problems, LANES)
            )
            for i in range(block)
            for j in range(i, block)
        }
        for j in range(block):
            scale = lax.rsqrt(entry[j, j])
            factor = {i: entry[j, i] * scale for i in range(j + 1, block)}
            hot = thin == offset + j
            panel[j] = [jnp.where(hot, 1.0, panel[j][0]) * scale] + [
                x * scale for x in panel[j][1:]
            ]
            for i in range(j + 1, block):
                for l in range(i, block):
                    entry[i, l] = entry[i, l] - factor[i] * factor[l]
                kept = [jnp.where(hot, 0.0, panel[i][0])] + panel[i][1:]
                panel[i] = [x - factor[i] * y for x, y in zip(kept, panel[j])]
            for x, t in zip(panel[j], order):
                tile_ref[t, pl.ds(base + j, problems, stride=width), :] = x
        after = base + block
        if after == width:
            continue
        first = after // LANES * LANES
        lane = iota((block, LANES), 1) - offset
        inverse = (lane < 0) | (lane >= block) | (lane <= iota((block, LANES), 0))
        below = iota((width - after, LANES), 1) - offset
        below = (below >= 0) & (below < block)
        for p in range(problems):
            start = p * width
            rows = [parts(tile_ref[t, start + base : start + after, :]) for t in range(tiles)]
            left = jnp.concatenate(
                [
                    jnp.concatenate([rows[t][q] for q in (0, 0, 1, 1, 0, 2)], 0)
                    for t in range(first // LANES, tiles)
                ],
                1,
            ).astype(jnp.bfloat16)
            rows[own] = [jnp.where(inverse, x, 0.0) for x in rows[own]]
            right = jnp.concatenate(
                [
                    jnp.concatenate([rows[t][q] for q in (0, 1, 0, 1, 2, 0)], 0)
                    for t in range(tiles)
                ],
                1,
            ).astype(jnp.bfloat16)
            update = lax.dot_general(
                left, right, (((0,), (0,)), ((), ())), preferred_element_type=jnp.float32
            )
            for t in range(tiles):
                old = tile_ref[t, start + after : start + width, :]
                if t == own:
                    old = jnp.where(below, 0.0, old)
                tile_ref[t, start + after : start + width, :] = (
                    old - update[after - first :, t * LANES : (t + 1) * LANES]
                )


def finish_kernel(
    place_ref,
    sample_ref,
    leaf_ref,
    pair_ref,
    group_ref,
    basis_ref,
    leaf_transfer_ref,
    pair_transfer_ref,
    group_factor_ref,
    tile_ref,
    upper_ref,
):
    width = sample_ref.shape[0]
    row = iota((LANES, LANES), 0)
    lane = iota((LANES, LANES), 1)
    for p, packed_ref in enumerate((leaf_ref, pair_ref, group_ref)):
        start = p * width
        shared = packed_ref[:LANES, :]
        tile_ref[0, start : start + LANES, :] = shared
        tile_ref[0, start + LANES : start + width, :] = jnp.zeros((LANES, LANES), jnp.float32)
        tile_ref[1, start : start + LANES, :] = packed_ref[LANES : 2 * LANES, :]
        diagonal = jnp.broadcast_to(packed_ref[2 * LANES : 2 * LANES + 1, :], (LANES, LANES))
        tile_ref[1, start + LANES : start + width, :] = jnp.where(
            lane == row, diagonal, shared.T
        )
    eliminate(tile_ref, 3, width, 16)
    row = iota((width, width), 0)
    lane = iota((width, width), 1)
    inverse = []
    for p in range(3):
        start = p * width
        whole = jnp.concatenate([tile_ref[t, start : start + width, :] for t in range(2)], 1)
        inverse.append(jnp.where(lane <= row, whole, 0.0))
        upper_ref[p] = jnp.where(
            lane > row, whole, jnp.where(lane == row, 1.0 / whole, 0.0)
        )
    basis_ref[...] = times_transpose(sample_ref[...].T, inverse[0])
    leaf_transfer_ref[...] = times_transpose(upper_ref[0], inverse[1])
    half = width // 2
    quarter = width // 4
    place = place_ref[0]
    pair_upper = upper_ref[1, pl.ds(pl.multiple_of(place % 2 * half, half), half), :]
    pair_transfer_ref[...] = times_transpose(pair_upper, inverse[2])
    group_factor_ref[...] = upper_ref[
        2, pl.ds(pl.multiple_of(place % 4 * quarter, quarter), quarter), :
    ]


def finish(place, sample_t, leaf, pair, group):
    width, rows = sample_t.shape
    shapes = [(rows, width), (width, width), (width // 2, width), (width // 4, width)]
    return pl.pallas_call(
        finish_kernel,
        out_shape=[jax.ShapeDtypeStruct(shape, jnp.float32) for shape in shapes],
        in_specs=[pl.BlockSpec(memory_space=pltpu.SMEM)]
        + [pl.BlockSpec(memory_space=pltpu.VMEM)] * 4,
        scratch_shapes=[
            pltpu.VMEM((width // LANES, 3 * width, LANES), jnp.float32),
            pltpu.VMEM((3, width, width), jnp.float32),
        ],
        compiler_params=pltpu.CompilerParams(vmem_limit_bytes=48 << 20),
        name="finish",
    )(place, sample_t, leaf, pair, group)


def local(probes, spectrum):
    devices = lax.axis_size("row") * lax.axis_size("col")
    axes = ("row", "col")
    columns = lax.all_to_all(
        spread(probes, spectrum, devices), axes, split_axis=0, concat_axis=0, tiled=True
    )
    moved = circulant(columns, probes.shape[0], devices)
    sample_t = lax.all_to_all(moved, axes, split_axis=0, concat_axis=0, tiled=True)
    leaf = packed_gram(sample_t)
    pair = leaf + partner(leaf, "col", 0)
    group = pair + partner(pair, "col", 1)
    place = lax.axis_index("col").reshape(1).astype(jnp.int32)
    return tuple(finish(place, sample_t, leaf, pair, group))


def solution(mesh):
    placed = P(("row", "col"), None)
    return jax.shard_map(
        local,
        mesh=mesh,
        in_specs=(placed, placed),
        out_specs=(placed, placed, placed, placed),
        check_vma=False,
    )
```

```python
import math

import jax
import jax.numpy as jnp
import numpy as np
from jax import lax
from jax.experimental import pallas as pl
from jax.experimental.pallas import tpu as pltpu
from jax.sharding import PartitionSpec as P

LANES = 128
HIGHEST = lax.Precision.HIGHEST


def partner(value, axis, distance):
    mask = 2**distance
    pairs = [(source, source ^ mask) for source in range(lax.axis_size(axis))]
    return lax.ppermute(value, axis, pairs)


def matmul(left, right):
    return jnp.dot(left, right, precision=HIGHEST, preferred_element_type=jnp.float32)


def circle(product, length):
    angle = 2.0 * np.pi / length * (product % length)
    return np.cos(angle), np.sin(angle)


def tables(devices, split):
    major = devices * split
    total = major * LANES
    order = (np.arange(devices)[None, :] * split + np.arange(split)[:, None]).reshape(-1)
    freq = np.arange(major)
    cos, sin = circle(freq[:, None] * order[None, :], major)
    first = np.block([[cos, sin], [-sin, cos]])
    lane = np.arange(LANES)
    cos, sin = circle(lane[:, None] * lane[None, :], LANES)
    second = np.block([[cos, -sin], [sin, cos]])
    cos_turn, sin_turn = circle(freq[:, None] * lane[None, :], total)
    turn = np.stack([cos_turn, sin_turn])
    return [np.asarray(t, np.float32) for t in (first, first.T, second, second.T, turn)]


def iota(shape, dim):
    return lax.broadcasted_iota(jnp.int32, shape, dim)


def times_transpose(left, right):
    return lax.dot_general(
        left,
        right,
        (((1,), (1,)), ((), ())),
        precision=HIGHEST,
        preferred_element_type=jnp.float32,
    )


def spread_kernel(per_dev, extra):
    def body(probes_ref, spectrum_ref, o_ref):
        rows, width = probes_ref.shape
        split = rows // LANES
        for j in range(split):
            lanes = slice(j * LANES, (j + 1) * LANES)
            o_ref[:, lanes] = probes_ref[lanes, :].T
        place = iota((LANES, rows), 1)
        own = jnp.where(place // split == iota((LANES, rows), 0), spectrum_ref[...], 0.0)
        for t in range(extra):
            part = iota((8, rows), 0) % per_dev + t * per_dev
            pick = jnp.where(iota((8, rows), 1) % split == part, 1.0, 0.0)
            symbol = times_transpose(pick, own)
            for r in range(0, width, 8):
                o_ref[r : r + 8, rows + t * LANES : rows + (t + 1) * LANES] = symbol

    return body


def spread(probes, spectrum, devices):
    rows, width = probes.shape
    per_dev = width // devices
    extra = pl.cdiv(rows // LANES, per_dev)
    return pl.pallas_call(
        spread_kernel(per_dev, extra),
        out_shape=jax.ShapeDtypeStruct((width, rows + extra * LANES), jnp.float32),
        name="spread",
    )(probes, spectrum)


def circulant_kernel(devices, split, per_dev, extra):
    major = devices * split
    pairs = per_dev // 2
    width = devices * per_dev

    def symmetric_symbol(tile_ref):
        lam = jnp.concatenate(
            [
                tile_ref[
                    pl.ds((split + h // per_dev) * width + h % per_dev, devices, stride=per_dev), :
                ]
                for h in range(split)
            ],
            0,
        )
        row = iota((LANES, LANES), 0)
        lane = iota((LANES, LANES), 1)
        flip = jnp.where(row + lane == LANES - 1, 1.0, 0.0)
        head_flip = jnp.where((row + lane) % LANES == 0, 1.0, 0.0)
        back = matmul(lam, jnp.concatenate([flip, head_flip], 1))
        row = iota((major, major), 0)
        lane = iota((major, major), 1)
        turn = jnp.where(row + lane == major, 1.0, 0.0)
        other = jnp.where(
            iota((major, LANES), 0) == 0, back[:, LANES:], matmul(turn, back[:, :LANES])
        )
        return (lam + other) * (0.5 / (major * LANES))

    def body(x_ref, first_ref, first_t_ref, second_ref, second_t_ref, turn_ref, o_ref, tile_ref):
        cos = turn_ref[0]
        sin = turn_ref[1]
        for j in range(split + extra):
            tile_ref[j * width : (j + 1) * width, :] = x_ref[:, j * LANES : (j + 1) * LANES]
        lam = symmetric_symbol(tile_ref)

        def column(c):
            return [
                tile_ref[pl.ds(j * width + c, devices, stride=per_dev), :] for j in range(split)
            ]

        packed = jnp.concatenate(
            [jnp.concatenate(column(2 * q) + column(2 * q + 1), 0) for q in range(pairs)], 1
        )
        mixed = matmul(first_ref[...], packed)
        turned = []
        for q in range(pairs):
            real = mixed[:major, q * LANES : (q + 1) * LANES]
            imag = mixed[major:, q * LANES : (q + 1) * LANES]
            turned.append(
                jnp.concatenate([real * cos + imag * sin, imag * cos - real * sin], 1)
            )
        spectra = matmul(jnp.concatenate(turned, 0), second_ref[...])
        lam = jnp.concatenate([lam, lam], 1)
        spectra = jnp.concatenate(
            [spectra[q * major : (q + 1) * major] * lam for q in range(pairs)], 0
        )
        back = matmul(spectra, second_t_ref[...])
        turned = []
        for q in range(pairs):
            real = back[q * major : (q + 1) * major, :LANES]
            imag = back[q * major : (q + 1) * major, LANES:]
            turned.append(
                jnp.concatenate([real * cos - imag * sin, imag * cos + real * sin], 0)
            )
        sample = matmul(first_t_ref[...], jnp.concatenate(turned, 1))
        for c in range(per_dev):
            for j in range(split):
                row = (c % 2) * major + j * devices
                lane = (c // 2) * LANES
                tile_ref[pl.ds(j * width + c, devices, stride=per_dev), :] = sample[
                    row : row + devices, lane : lane + LANES
                ]
        for j in range(split):
            o_ref[:, j * LANES : (j + 1) * LANES] = tile_ref[j * width : (j + 1) * width, :]

    return body


def circulant(columns, rows, devices):
    width = columns.shape[0]
    split = rows // LANES
    tiles = columns.shape[1] // LANES
    return pl.pallas_call(
        circulant_kernel(devices, split, width // devices, tiles - split),
        out_shape=jax.ShapeDtypeStruct((width, rows), jnp.float32),
        scratch_shapes=[pltpu.VMEM((tiles * width, LANES), jnp.float32)],
        compiler_params=pltpu.CompilerParams(vmem_limit_bytes=48 << 20),
        name="circulant",
    )(columns, *tables(devices, split))


def gram_kernel(sample_ref, packed_ref):
    width, rows = sample_ref.shape
    upper = times_transpose(sample_ref[:LANES, :], sample_ref[...]) * (1.0 / rows)
    last = sample_ref[LANES:, :]
    last = times_transpose(last, last) * (1.0 / rows)
    row = iota((LANES, LANES), 0)
    lane = iota((LANES, LANES), 1)
    packed_ref[:LANES, :] = jnp.where(lane >= row, upper[:, :LANES], last)
    packed_ref[LANES : 2 * LANES, :] = upper[:, LANES:]
    diagonal = jnp.sum(jnp.where(lane == row, last, 0.0), axis=0, keepdims=True)
    packed_ref[2 * LANES :, :] = jnp.broadcast_to(diagonal, (8, LANES))


def packed_gram(sample_t):
    return pl.pallas_call(
        gram_kernel,
        out_shape=jax.ShapeDtypeStruct((2 * LANES + 8, LANES), jnp.float32),
        name="gram",
    )(sample_t)


def parts(value):
    high = value.astype(jnp.bfloat16).astype(jnp.float32)
    rest = value - high
    middle = rest.astype(jnp.bfloat16).astype(jnp.float32)
    return high, middle, rest - middle


def eliminate(tile_ref, done_ref, problems, width, block):
    tiles = width // LANES
    thin = iota((problems, LANES), 1)

    def across(value, lane):
        return jnp.broadcast_to(value[:, lane : lane + 1], (problems, LANES))

    def load(base):
        return [
            [tile_ref[t, pl.ds(base + i, problems, stride=width), :] for t in range(tiles)]
            for i in range(block)
        ]

    panel = load(0)
    for base in range(0, width, block):
        own, offset = divmod(base, LANES)
        entry = {
            (i, j): across(panel[i][own], offset + j)
            for i in range(block)
            for j in range(i, block)
        }
        for j in range(block):
            scale = lax.rsqrt(entry[j, j])
            factor = {i: entry[j, i] * scale for i in range(j + 1, block)}
            hot = thin == offset + j
            panel[j][own] = jnp.where(hot, 1.0, panel[j][own])
            panel[j] = [x * scale for x in panel[j]]
            for i in range(j + 1, block):
                for l in range(i, block):
                    entry[i, l] = entry[i, l] - factor[i] * factor[l]
                panel[i][own] = jnp.where(hot, 0.0, panel[i][own])
                panel[i] = [x - factor[i] * y for x, y in zip(panel[i], panel[j])]
            for t in range(tiles):
                done_ref[t, pl.ds(base + j, problems, stride=width), :] = panel[j][t]
        after = base + block
        if after == width:
            break
        inside = (thin >= offset) & (thin < offset + block)
        clean = [list(rows) for rows in panel]
        for j in range(block):
            clean[j][own] = jnp.where(inside & (thin > offset + j), 0.0, panel[j][own])
        ahead = load(after)
        for i in range(block):
            ahead[i][own] = jnp.where(inside, 0.0, ahead[i][own])
            for j in range(block):
                weight = across(panel[j][after // LANES], after % LANES + i)
                ahead[i] = [x - weight * y for x, y in zip(ahead[i], clean[j])]
        panel = ahead
        past = after + block
        if past == width:
            continue
        first = past // LANES
        lane = iota((block, LANES), 1) - offset
        inverse = (lane < 0) | (lane >= block) | (lane <= iota((block, LANES), 0))
        below = iota((width - past, LANES), 1) - offset
        below = (below >= 0) & (below < block)
        for p in range(problems):
            start = p * width
            rows = [parts(done_ref[t, start + base : start + after, :]) for t in range(tiles)]
            left = jnp.concatenate(
                [
                    jnp.concatenate([rows[t][q] for q in (0, 0, 1, 1, 0, 2)], 0)
                    for t in range(first, tiles)
                ],
                1,
            ).astype(jnp.bfloat16)
            rows[own] = [jnp.where(inverse, x, 0.0) for x in rows[own]]
            right = jnp.concatenate(
                [
                    jnp.concatenate([rows[t][q] for q in (0, 1, 0, 1, 2, 0)], 0)
                    for t in range(tiles)
                ],
                1,
            ).astype(jnp.bfloat16)
            update = lax.dot_general(
                left, right, (((0,), (0,)), ((), ())), preferred_element_type=jnp.float32
            )
            for t in range(tiles):
                old = tile_ref[t, start + past : start + width, :]
                if t == own:
                    old = jnp.where(below, 0.0, old)
                tile_ref[t, start + past : start + width, :] = (
                    old - update[past - first * LANES :, t * LANES : (t + 1) * LANES]
                )


def finish_kernel(
    place_ref,
    sample_ref,
    leaf_ref,
    pair_ref,
    group_ref,
    basis_ref,
    leaf_transfer_ref,
    pair_transfer_ref,
    group_factor_ref,
    tile_ref,
    done_ref,
    upper_ref,
):
    width = sample_ref.shape[0]
    row = iota((LANES, LANES), 0)
    lane = iota((LANES, LANES), 1)
    for p, packed_ref in enumerate((leaf_ref, pair_ref, group_ref)):
        start = p * width
        shared = packed_ref[:LANES, :]
        tile_ref[0, start : start + LANES, :] = shared
        tile_ref[0, start + LANES : start + width, :] = jnp.zeros((LANES, LANES), jnp.float32)
        tile_ref[1, start : start + LANES, :] = packed_ref[LANES : 2 * LANES, :]
        diagonal = jnp.broadcast_to(packed_ref[2 * LANES : 2 * LANES + 1, :], (LANES, LANES))
        tile_ref[1, start + LANES : start + width, :] = jnp.where(
            lane == row, diagonal, shared.T
        )
    eliminate(tile_ref, done_ref, 3, width, 8)
    row = iota((width, width), 0)
    lane = iota((width, width), 1)
    inverse = []
    for p in range(3):
        start = p * width
        whole = jnp.concatenate([done_ref[t, start : start + width, :] for t in range(2)], 1)
        inverse.append(jnp.where(lane <= row, whole, 0.0))
        upper_ref[p] = jnp.where(
            lane > row, whole, jnp.where(lane == row, 1.0 / whole, 0.0)
        )
    basis_ref[...] = times_transpose(sample_ref[...].T, inverse[0])
    leaf_transfer_ref[...] = times_transpose(upper_ref[0], inverse[1])
    half = width // 2
    quarter = width // 4
    place = place_ref[0]
    pair_upper = upper_ref[1, pl.ds(pl.multiple_of(place % 2 * half, half), half), :]
    pair_transfer_ref[...] = times_transpose(pair_upper, inverse[2])
    group_factor_ref[...] = upper_ref[
        2, pl.ds(pl.multiple_of(place % 4 * quarter, quarter), quarter), :
    ]


def finish(place, sample_t, leaf, pair, group):
    width, rows = sample_t.shape
    shapes = [(rows, width), (width, width), (width // 2, width), (width // 4, width)]
    return pl.pallas_call(
        finish_kernel,
        out_shape=[jax.ShapeDtypeStruct(shape, jnp.float32) for shape in shapes],
        in_specs=[pl.BlockSpec(memory_space=pltpu.SMEM)]
        + [pl.BlockSpec(memory_space=pltpu.VMEM)] * 4,
        scratch_shapes=[
            pltpu.VMEM((width // LANES, 3 * width, LANES), jnp.float32),
            pltpu.VMEM((width // LANES, 3 * width, LANES), jnp.float32),
            pltpu.VMEM((3, width, width), jnp.float32),
        ],
        compiler_params=pltpu.CompilerParams(vmem_limit_bytes=48 << 20),
        name="finish",
    )(place, sample_t, leaf, pair, group)


def local(probes, spectrum):
    devices = lax.axis_size("row") * lax.axis_size("col")
    axes = ("row", "col")
    columns = lax.all_to_all(
        spread(probes, spectrum, devices), axes, split_axis=0, concat_axis=0, tiled=True
    )
    moved = circulant(columns, probes.shape[0], devices)
    sample_t = lax.all_to_all(moved, axes, split_axis=0, concat_axis=0, tiled=True)
    leaf = packed_gram(sample_t)
    pair = leaf + partner(leaf, "col", 0)
    group = pair + partner(pair, "col", 1)
    place = lax.axis_index("col").reshape(1).astype(jnp.int32)
    return tuple(finish(place, sample_t, leaf, pair, group))


def solution(mesh):
    placed = P(("row", "col"), None)
    return jax.shard_map(
        local,
        mesh=mesh,
        in_specs=(placed, placed),
        out_specs=(placed, placed, placed, placed),
        check_vma=False,
    )
```

```python
import math

import jax
import jax.numpy as jnp
import numpy as np
from jax import lax
from jax.experimental import pallas as pl
from jax.experimental.pallas import tpu as pltpu
from jax.sharding import PartitionSpec as P

LANES = 128
HIGHEST = lax.Precision.HIGHEST


def partner(value, axis, mask):
    pairs = [(source, source ^ mask) for source in range(lax.axis_size(axis))]
    return lax.ppermute(value, axis, pairs)


def matmul(left, right):
    return jnp.dot(left, right, precision=HIGHEST, preferred_element_type=jnp.float32)


def circle(product, length):
    angle = 2.0 * np.pi / length * (product % length)
    return np.cos(angle), np.sin(angle)


def tables(devices, split):
    major = devices * split
    total = major * LANES
    order = (np.arange(devices)[None, :] * split + np.arange(split)[:, None]).reshape(-1)
    freq = np.arange(major)
    cos, sin = circle(freq[:, None] * order[None, :], major)
    first = np.block([[cos, sin], [-sin, cos]])
    lane = np.arange(LANES)
    cos, sin = circle(lane[:, None] * lane[None, :], LANES)
    second = np.block([[cos, -sin], [sin, cos]])
    cos_turn, sin_turn = circle(freq[:, None] * lane[None, :], total)
    turn = np.stack([cos_turn, sin_turn])
    return [np.asarray(t, np.float32) for t in (first, first.T, second, second.T, turn)]


def iota(shape, dim):
    return lax.broadcasted_iota(jnp.int32, shape, dim)


def times_transpose(left, right):
    return lax.dot_general(
        left,
        right,
        (((1,), (1,)), ((), ())),
        precision=HIGHEST,
        preferred_element_type=jnp.float32,
    )


def spread_kernel(per_dev, extra):
    def body(probes_ref, spectrum_ref, o_ref):
        rows, width = probes_ref.shape
        split = rows // LANES
        for j in range(split):
            lanes = slice(j * LANES, (j + 1) * LANES)
            o_ref[:, lanes] = probes_ref[lanes, :].T
        place = iota((LANES, rows), 1)
        own = jnp.where(place // split == iota((LANES, rows), 0), spectrum_ref[...], 0.0)
        for t in range(extra):
            part = iota((8, rows), 0) % per_dev + t * per_dev
            pick = jnp.where(iota((8, rows), 1) % split == part, 1.0, 0.0)
            symbol = times_transpose(pick, own)
            for r in range(0, width, 8):
                o_ref[r : r + 8, rows + t * LANES : rows + (t + 1) * LANES] = symbol

    return body


def spread(probes, spectrum, devices):
    rows, width = probes.shape
    per_dev = width // devices
    extra = pl.cdiv(rows // LANES, per_dev)
    return pl.pallas_call(
        spread_kernel(per_dev, extra),
        out_shape=jax.ShapeDtypeStruct((width, rows + extra * LANES), jnp.float32),
        name="spread",
    )(probes, spectrum)


def circulant_kernel(devices, split, per_dev, extra):
    major = devices * split
    pairs = per_dev // 2
    width = devices * per_dev

    def symmetric_symbol(tile_ref):
        lam = jnp.concatenate(
            [
                tile_ref[
                    pl.ds((split + h // per_dev) * width + h % per_dev, devices, stride=per_dev), :
                ]
                for h in range(split)
            ],
            0,
        )
        row = iota((LANES, LANES), 0)
        lane = iota((LANES, LANES), 1)
        flip = jnp.where(row + lane == LANES - 1, 1.0, 0.0)
        head_flip = jnp.where((row + lane) % LANES == 0, 1.0, 0.0)
        back = matmul(lam, jnp.concatenate([flip, head_flip], 1))
        row = iota((major, major), 0)
        lane = iota((major, major), 1)
        turn = jnp.where(row + lane == major, 1.0, 0.0)
        other = jnp.where(
            iota((major, LANES), 0) == 0, back[:, LANES:], matmul(turn, back[:, :LANES])
        )
        return (lam + other) * (0.5 / (major * LANES))

    def body(x_ref, first_ref, first_t_ref, second_ref, second_t_ref, turn_ref, o_ref, tile_ref):
        cos = turn_ref[0]
        sin = turn_ref[1]
        for j in range(split + extra):
            tile_ref[j * width : (j + 1) * width, :] = x_ref[:, j * LANES : (j + 1) * LANES]
        lam = symmetric_symbol(tile_ref)

        def column(c):
            return [
                tile_ref[pl.ds(j * width + c, devices, stride=per_dev), :] for j in range(split)
            ]

        packed = jnp.concatenate(
            [jnp.concatenate(column(2 * q) + column(2 * q + 1), 0) for q in range(pairs)], 1
        )
        mixed = matmul(first_ref[...], packed)
        turned = []
        for q in range(pairs):
            real = mixed[:major, q * LANES : (q + 1) * LANES]
            imag = mixed[major:, q * LANES : (q + 1) * LANES]
            turned.append(
                jnp.concatenate([real * cos + imag * sin, imag * cos - real * sin], 1)
            )
        spectra = matmul(jnp.concatenate(turned, 0), second_ref[...])
        lam = jnp.concatenate([lam, lam], 1)
        spectra = jnp.concatenate(
            [spectra[q * major : (q + 1) * major] * lam for q in range(pairs)], 0
        )
        back = matmul(spectra, second_t_ref[...])
        turned = []
        for q in range(pairs):
            real = back[q * major : (q + 1) * major, :LANES]
            imag = back[q * major : (q + 1) * major, LANES:]
            turned.append(
                jnp.concatenate([real * cos - imag * sin, imag * cos + real * sin], 0)
            )
        sample = matmul(first_t_ref[...], jnp.concatenate(turned, 1))
        for c in range(per_dev):
            for j in range(split):
                row = (c % 2) * major + j * devices
                lane = (c // 2) * LANES
                tile_ref[pl.ds(j * width + c, devices, stride=per_dev), :] = sample[
                    row : row + devices, lane : lane + LANES
                ]
        for j in range(split):
            o_ref[:, j * LANES : (j + 1) * LANES] = tile_ref[j * width : (j + 1) * width, :]

    return body


def circulant(columns, rows, devices):
    width = columns.shape[0]
    split = rows // LANES
    tiles = columns.shape[1] // LANES
    return pl.pallas_call(
        circulant_kernel(devices, split, width // devices, tiles - split),
        out_shape=jax.ShapeDtypeStruct((width, rows), jnp.float32),
        scratch_shapes=[pltpu.VMEM((tiles * width, LANES), jnp.float32)],
        compiler_params=pltpu.CompilerParams(vmem_limit_bytes=48 << 20),
        name="circulant",
    )(columns, *tables(devices, split))


def packed_gram(sample_t):
    gram = times_transpose(sample_t, sample_t) * (1.0 / sample_t.shape[1])
    row = iota((LANES, LANES), 0)
    lane = iota((LANES, LANES), 1)
    last = gram[LANES:, LANES:]
    shared = jnp.where(lane >= row, gram[:LANES, :LANES], last)
    diagonal = jnp.sum(jnp.where(lane == row, last, 0.0), axis=0, keepdims=True)
    return jnp.concatenate(
        [shared, gram[:LANES, LANES:], jnp.broadcast_to(diagonal, (8, LANES))], 0
    )


def parts(value):
    high = value.astype(jnp.bfloat16).astype(jnp.float32)
    rest = value - high
    middle = rest.astype(jnp.bfloat16).astype(jnp.float32)
    return high, middle, rest - middle


def eliminate(tile_ref, done_ref, problems, width, block):
    tiles = width // LANES
    thin = iota((problems, LANES), 1)

    def across(value, lane):
        return jnp.broadcast_to(value[:, lane : lane + 1], (problems, LANES))

    def load(base):
        return [
            [tile_ref[t, pl.ds(base + i, problems, stride=width), :] for t in range(tiles)]
            for i in range(block)
        ]

    panel = load(0)
    for base in range(0, width, block):
        own, offset = divmod(base, LANES)
        entry = {
            (i, j): across(panel[i][own], offset + j)
            for i in range(block)
            for j in range(i, block)
        }
        for j in range(block):
            scale = lax.rsqrt(entry[j, j])
            factor = {i: entry[j, i] * scale for i in range(j + 1, block)}
            hot = thin == offset + j
            panel[j][own] = jnp.where(hot, 1.0, panel[j][own])
            panel[j] = [x * scale for x in panel[j]]
            for i in range(j + 1, block):
                for l in range(i, block):
                    entry[i, l] = entry[i, l] - factor[i] * factor[l]
                panel[i][own] = jnp.where(hot, 0.0, panel[i][own])
                panel[i] = [x - factor[i] * y for x, y in zip(panel[i], panel[j])]
            for t in range(tiles):
                done_ref[t, pl.ds(base + j, problems, stride=width), :] = panel[j][t]
        after = base + block
        if after == width:
            break
        inside = (thin >= offset) & (thin < offset + block)
        clean = [list(rows) for rows in panel]
        for j in range(block):
            clean[j][own] = jnp.where(inside & (thin > offset + j), 0.0, panel[j][own])
        ahead = load(after)
        for i in range(block):
            ahead[i][own] = jnp.where(inside, 0.0, ahead[i][own])
            for j in range(block):
                weight = across(panel[j][after // LANES], after % LANES + i)
                ahead[i] = [x - weight * y for x, y in zip(ahead[i], clean[j])]
        panel = ahead
        past = after + block
        if past == width:
            continue
        first = past // LANES
        lane = iota((block, LANES), 1) - offset
        inverse = (lane < 0) | (lane >= block) | (lane <= iota((block, LANES), 0))
        below = iota((width - past, LANES), 1) - offset
        below = (below >= 0) & (below < block)
        for p in range(problems):
            start = p * width
            rows = [parts(done_ref[t, start + base : start + after, :]) for t in range(tiles)]
            left = jnp.concatenate(
                [
                    jnp.concatenate([rows[t][q] for q in (0, 0, 1, 1, 0, 2)], 0)
                    for t in range(first, tiles)
                ],
                1,
            ).astype(jnp.bfloat16)
            rows[own] = [jnp.where(inverse, x, 0.0) for x in rows[own]]
            right = jnp.concatenate(
                [
                    jnp.concatenate([rows[t][q] for q in (0, 1, 0, 1, 2, 0)], 0)
                    for t in range(tiles)
                ],
                1,
            ).astype(jnp.bfloat16)
            update = lax.dot_general(
                left, right, (((0,), (0,)), ((), ())), preferred_element_type=jnp.float32
            )
            for t in range(tiles):
                old = tile_ref[t, start + past : start + width, :]
                if t == own:
                    old = jnp.where(below, 0.0, old)
                tile_ref[t, start + past : start + width, :] = (
                    old - update[past - first * LANES :, t * LANES : (t + 1) * LANES]
                )


def unpack(packed, tile_ref, start, width):
    row = iota((LANES, LANES), 0)
    lane = iota((LANES, LANES), 1)
    shared = packed[:LANES, :]
    tile_ref[0, start : start + LANES, :] = shared
    tile_ref[0, start + LANES : start + width, :] = jnp.zeros((LANES, LANES), jnp.float32)
    tile_ref[1, start : start + LANES, :] = packed[LANES : 2 * LANES, :]
    diagonal = jnp.broadcast_to(packed[2 * LANES : 2 * LANES + 1, :], (LANES, LANES))
    tile_ref[1, start + LANES : start + width, :] = jnp.where(lane == row, diagonal, shared.T)


def factors(done_ref, start, width):
    row = iota((width, width), 0)
    lane = iota((width, width), 1)
    whole = jnp.concatenate([done_ref[t, start : start + width, :] for t in range(2)], 1)
    upper = jnp.where(lane > row, whole, jnp.where(lane == row, 1.0 / whole, 0.0))
    return upper, jnp.where(lane <= row, whole, 0.0)


def leaf_kernel(sample_ref, packed_ref, basis_ref, upper_ref, tile_ref, done_ref):
    width = sample_ref.shape[0]
    unpack(packed_ref[...], tile_ref, 0, width)
    eliminate(tile_ref, done_ref, 1, width, 8)
    upper, inverse = factors(done_ref, 0, width)
    upper_ref[...] = upper
    basis_ref[...] = times_transpose(sample_ref[...].T, inverse)


def group_kernel(
    place_ref,
    leaf_ref,
    near_ref,
    far_ref,
    last_ref,
    leaf_upper_ref,
    leaf_transfer_ref,
    pair_transfer_ref,
    group_factor_ref,
    tile_ref,
    done_ref,
    upper_ref,
):
    width = leaf_upper_ref.shape[0]
    pair = leaf_ref[...] + near_ref[...]
    unpack(pair, tile_ref, 0, width)
    unpack(pair + (far_ref[...] + last_ref[...]), tile_ref, width, width)
    eliminate(tile_ref, done_ref, 2, width, 8)
    upper_ref[0], pair_inverse = factors(done_ref, 0, width)
    upper_ref[1], group_inverse = factors(done_ref, width, width)
    leaf_transfer_ref[...] = times_transpose(leaf_upper_ref[...], pair_inverse)
    half = width // 2
    quarter = width // 4
    place = place_ref[0]
    pair_upper = upper_ref[0, pl.ds(pl.multiple_of(place % 2 * half, half), half), :]
    pair_transfer_ref[...] = times_transpose(pair_upper, group_inverse)
    group_factor_ref[...] = upper_ref[
        1, pl.ds(pl.multiple_of(place % 4 * quarter, quarter), quarter), :
    ]


def scratch(problems, width):
    tiles = width // LANES
    return [pltpu.VMEM((tiles, problems * width, LANES), jnp.float32)] * 2


def leaf_factor(sample_t, leaf):
    width, rows = sample_t.shape
    return pl.pallas_call(
        leaf_kernel,
        out_shape=[jax.ShapeDtypeStruct(shape, jnp.float32) for shape in ((rows, width), (width, width))],
        scratch_shapes=scratch(1, width),
        compiler_params=pltpu.CompilerParams(vmem_limit_bytes=24 << 20),
        name="leaf",
    )(sample_t, leaf)


def group_factors(place, leaf, near, far, last, leaf_upper):
    width = leaf_upper.shape[0]
    shapes = [(width, width), (width // 2, width), (width // 4, width)]
    return pl.pallas_call(
        group_kernel,
        out_shape=[jax.ShapeDtypeStruct(shape, jnp.float32) for shape in shapes],
        in_specs=[pl.BlockSpec(memory_space=pltpu.SMEM)]
        + [pl.BlockSpec(memory_space=pltpu.VMEM)] * 5,
        scratch_shapes=scratch(2, width) + [pltpu.VMEM((2, width, width), jnp.float32)],
        compiler_params=pltpu.CompilerParams(vmem_limit_bytes=24 << 20),
        name="group",
    )(place, leaf, near, far, last, leaf_upper)


def local(probes, spectrum):
    devices = lax.axis_size("row") * lax.axis_size("col")
    axes = ("row", "col")
    columns = lax.all_to_all(
        spread(probes, spectrum, devices), axes, split_axis=0, concat_axis=0, tiled=True
    )
    moved = circulant(columns, probes.shape[0], devices)
    sample_t = lax.all_to_all(moved, axes, split_axis=0, concat_axis=0, tiled=True)
    leaf = packed_gram(sample_t)
    near, far, last = (partner(leaf, "col", mask) for mask in (1, 2, 3))
    leaf_basis, leaf_upper = leaf_factor(sample_t, leaf)
    place = lax.axis_index("col").reshape(1).astype(jnp.int32)
    return (leaf_basis, *group_factors(place, leaf, near, far, last, leaf_upper))


def solution(mesh):
    placed = P(("row", "col"), None)
    return jax.shard_map(
        local,
        mesh=mesh,
        in_specs=(placed, placed),
        out_specs=(placed, placed, placed, placed),
        check_vma=False,
    )
```

```python
import math

import jax
import jax.numpy as jnp
import numpy as np
from jax import lax
from jax.experimental import pallas as pl
from jax.experimental.pallas import tpu as pltpu
from jax.sharding import PartitionSpec as P

LANES = 128
HIGHEST = lax.Precision.HIGHEST


def partner(value, axis, mask):
    pairs = [(source, source ^ mask) for source in range(lax.axis_size(axis))]
    return lax.ppermute(value, axis, pairs)


def matmul(left, right):
    return jnp.dot(left, right, precision=HIGHEST, preferred_element_type=jnp.float32)


def circle(product, length):
    angle = 2.0 * np.pi / length * (product % length)
    return np.cos(angle), np.sin(angle)


def tables(devices, split):
    major = devices * split
    total = major * LANES
    order = (np.arange(devices)[None, :] * split + np.arange(split)[:, None]).reshape(-1)
    freq = np.arange(major)
    cos, sin = circle(freq[:, None] * order[None, :], major)
    first = np.block([[cos, sin], [-sin, cos]])
    lane = np.arange(LANES)
    cos, sin = circle(lane[:, None] * lane[None, :], LANES)
    second = np.block([[cos, -sin], [sin, cos]])
    cos_turn, sin_turn = circle(freq[:, None] * lane[None, :], total)
    turn = np.stack([cos_turn, sin_turn])
    return [np.asarray(t, np.float32) for t in (first, first.T, second, second.T, turn)]


def iota(shape, dim):
    return lax.broadcasted_iota(jnp.int32, shape, dim)


def times_transpose(left, right):
    return lax.dot_general(
        left,
        right,
        (((1,), (1,)), ((), ())),
        precision=HIGHEST,
        preferred_element_type=jnp.float32,
    )


def spread_kernel(per_dev, extra):
    def body(probes_ref, spectrum_ref, o_ref):
        rows, width = probes_ref.shape
        split = rows // LANES
        for j in range(split):
            lanes = slice(j * LANES, (j + 1) * LANES)
            o_ref[:, lanes] = probes_ref[lanes, :].T
        place = iota((LANES, rows), 1)
        own = jnp.where(place // split == iota((LANES, rows), 0), spectrum_ref[...], 0.0)
        for t in range(extra):
            part = iota((8, rows), 0) % per_dev + t * per_dev
            pick = jnp.where(iota((8, rows), 1) % split == part, 1.0, 0.0)
            symbol = times_transpose(pick, own)
            for r in range(0, width, 8):
                o_ref[r : r + 8, rows + t * LANES : rows + (t + 1) * LANES] = symbol

    return body


def spread(probes, spectrum, devices):
    rows, width = probes.shape
    per_dev = width // devices
    extra = pl.cdiv(rows // LANES, per_dev)
    return pl.pallas_call(
        spread_kernel(per_dev, extra),
        out_shape=jax.ShapeDtypeStruct((width, rows + extra * LANES), jnp.float32),
        name="spread",
    )(probes, spectrum)


def circulant_kernel(devices, split, per_dev, extra):
    major = devices * split
    pairs = per_dev // 2
    width = devices * per_dev

    def symmetric_symbol(tile_ref):
        lam = jnp.concatenate(
            [
                tile_ref[
                    pl.ds((split + h // per_dev) * width + h % per_dev, devices, stride=per_dev), :
                ]
                for h in range(split)
            ],
            0,
        )
        row = iota((LANES, LANES), 0)
        lane = iota((LANES, LANES), 1)
        flip = jnp.where(row + lane == LANES - 1, 1.0, 0.0)
        head_flip = jnp.where((row + lane) % LANES == 0, 1.0, 0.0)
        back = matmul(lam, jnp.concatenate([flip, head_flip], 1))
        row = iota((major, major), 0)
        lane = iota((major, major), 1)
        turn = jnp.where(row + lane == major, 1.0, 0.0)
        other = jnp.where(
            iota((major, LANES), 0) == 0, back[:, LANES:], matmul(turn, back[:, :LANES])
        )
        return (lam + other) * (0.5 / (major * LANES))

    def body(x_ref, first_ref, first_t_ref, second_ref, second_t_ref, turn_ref, o_ref, tile_ref):
        cos = turn_ref[0]
        sin = turn_ref[1]
        for j in range(split + extra):
            tile_ref[j * width : (j + 1) * width, :] = x_ref[:, j * LANES : (j + 1) * LANES]
        lam = symmetric_symbol(tile_ref)

        def column(c):
            return [
                tile_ref[pl.ds(j * width + c, devices, stride=per_dev), :] for j in range(split)
            ]

        packed = jnp.concatenate(
            [jnp.concatenate(column(2 * q) + column(2 * q + 1), 0) for q in range(pairs)], 1
        )
        mixed = matmul(first_ref[...], packed)
        turned = []
        for q in range(pairs):
            real = mixed[:major, q * LANES : (q + 1) * LANES]
            imag = mixed[major:, q * LANES : (q + 1) * LANES]
            turned.append(
                jnp.concatenate([real * cos + imag * sin, imag * cos - real * sin], 1)
            )
        spectra = matmul(jnp.concatenate(turned, 0), second_ref[...])
        lam = jnp.concatenate([lam, lam], 1)
        spectra = jnp.concatenate(
            [spectra[q * major : (q + 1) * major] * lam for q in range(pairs)], 0
        )
        back = matmul(spectra, second_t_ref[...])
        turned = []
        for q in range(pairs):
            real = back[q * major : (q + 1) * major, :LANES]
            imag = back[q * major : (q + 1) * major, LANES:]
            turned.append(
                jnp.concatenate([real * cos - imag * sin, imag * cos + real * sin], 0)
            )
        sample = matmul(first_t_ref[...], jnp.concatenate(turned, 1))
        for c in range(per_dev):
            for j in range(split):
                row = (c % 2) * major + j * devices
                lane = (c // 2) * LANES
                tile_ref[pl.ds(j * width + c, devices, stride=per_dev), :] = sample[
                    row : row + devices, lane : lane + LANES
                ]
        for j in range(split):
            o_ref[:, j * LANES : (j + 1) * LANES] = tile_ref[j * width : (j + 1) * width, :]

    return body


def circulant(columns, rows, devices):
    width = columns.shape[0]
    split = rows // LANES
    tiles = columns.shape[1] // LANES
    return pl.pallas_call(
        circulant_kernel(devices, split, width // devices, tiles - split),
        out_shape=jax.ShapeDtypeStruct((width, rows), jnp.float32),
        scratch_shapes=[pltpu.VMEM((tiles * width, LANES), jnp.float32)],
        compiler_params=pltpu.CompilerParams(vmem_limit_bytes=48 << 20),
        name="circulant",
    )(columns, *tables(devices, split))


def packed_gram(sample_t):
    gram = times_transpose(sample_t, sample_t) * (1.0 / sample_t.shape[1])
    row = iota((LANES, LANES), 0)
    lane = iota((LANES, LANES), 1)
    last = gram[LANES:, LANES:]
    shared = jnp.where(lane >= row, gram[:LANES, :LANES], last)
    diagonal = jnp.sum(jnp.where(lane == row, last, 0.0), axis=0, keepdims=True)
    return jnp.concatenate(
        [shared, gram[:LANES, LANES:], jnp.broadcast_to(diagonal, (8, LANES))], 0
    )


def parts(value):
    high = value.astype(jnp.bfloat16).astype(jnp.float32)
    rest = value - high
    middle = rest.astype(jnp.bfloat16).astype(jnp.float32)
    return high, middle, rest - middle


def eliminate(tile_ref, done_ref, problems, width):
    tiles = width // LANES
    block = 8
    shape = (block, LANES)
    sub = iota(shape, 0)
    lane = iota(shape, 1)

    def row_of(value, i):
        return jnp.broadcast_to(value[i : i + 1, :], shape)

    def lane_of(value, l):
        return jnp.broadcast_to(value[:, l : l + 1], shape)

    def turned(value, l):
        only = jnp.sum(jnp.where(lane == sub + l, value, 0.0), axis=1, keepdims=True)
        return jnp.broadcast_to(only, shape)

    def load(base):
        return [
            [
                tile_ref[t, p * width + base : p * width + base + block, :]
                for t in range(tiles)
            ]
            for p in range(problems)
        ]

    panel = load(0)
    for base in range(0, width, block):
        own, offset = divmod(base, LANES)
        after = base + block
        more = after < width
        column = [[lane_of(x[own], offset + l) for l in range(block)] for x in panel]
        inside = (lane >= offset) & (lane < offset + block)
        if more:
            near, shift = divmod(after, LANES)
            cross = [[turned(row_of(x[near], i), shift) for i in range(block)] for x in panel]
            ahead = load(after)
            for x in ahead:
                x[own] = jnp.where(inside, 0.0, x[own])
        for j in range(block):
            hot = (lane == offset + j) & (sub >= j)
            unit = jnp.where(sub == j, 1.0, 0.0)
            for p in range(problems):
                x, c = panel[p], column[p]
                scale = lax.rsqrt(row_of(c[j], j))
                factor = c[j] * scale
                each = {l: row_of(factor, l) for l in range(j + 1, block)}
                for l in range(j + 1, block):
                    c[l] = c[l] - factor * each[l]
                lower = jnp.where(sub > j, factor, 0.0)
                x[own] = jnp.where(hot, unit, x[own])
                pivot = [row_of(y, j) * scale for y in x]
                panel[p] = [
                    jnp.where(sub == j, v, y - lower * v) for v, y in zip(pivot, x)
                ]
                if more:
                    weight = cross[p][j] * scale
                    for i in range(j + 1, block):
                        cross[p][i] = cross[p][i] - each[i] * weight
                    pivot[own] = jnp.where(inside & (lane > offset + j), 0.0, pivot[own])
                    ahead[p] = [y - weight * v for v, y in zip(pivot, ahead[p])]
        for p in range(problems):
            for t in range(tiles):
                done_ref[t, p * width + base : p * width + after, :] = panel[p][t]
        if not more:
            break
        done, panel = panel, ahead
        past = after + block
        if past == width:
            continue
        first = past // LANES
        inverse = ~inside | (lane - offset <= sub)
        below = iota((width - past, LANES), 1) - offset
        below = (below >= 0) & (below < block)
        for p in range(problems):
            start = p * width
            rows = [parts(x) for x in done[p]]
            left = jnp.concatenate(
                [
                    jnp.concatenate([rows[t][q] for q in (0, 0, 1, 1, 0, 2)], 0)
                    for t in range(first, tiles)
                ],
                1,
            ).astype(jnp.bfloat16)
            rows[own] = [jnp.where(inverse, x, 0.0) for x in rows[own]]
            right = jnp.concatenate(
                [
                    jnp.concatenate([rows[t][q] for q in (0, 1, 0, 1, 2, 0)], 0)
                    for t in range(tiles)
                ],
                1,
            ).astype(jnp.bfloat16)
            update = lax.dot_general(
                left, right, (((0,), (0,)), ((), ())), preferred_element_type=jnp.float32
            )
            for t in range(tiles):
                old = tile_ref[t, start + past : start + width, :]
                if t == own:
                    old = jnp.where(below, 0.0, old)
                tile_ref[t, start + past : start + width, :] = (
                    old - update[past - first * LANES :, t * LANES : (t + 1) * LANES]
                )


def unpack(packed, tile_ref, start, width):
    row = iota((LANES, LANES), 0)
    lane = iota((LANES, LANES), 1)
    shared = packed[:LANES, :]
    other = shared.T
    tile_ref[0, start : start + LANES, :] = jnp.where(lane >= row, shared, other)
    tile_ref[0, start + LANES : start + width, :] = jnp.zeros((LANES, LANES), jnp.float32)
    tile_ref[1, start : start + LANES, :] = packed[LANES : 2 * LANES, :]
    diagonal = jnp.broadcast_to(packed[2 * LANES : 2 * LANES + 1, :], (LANES, LANES))
    tile_ref[1, start + LANES : start + width, :] = jnp.where(
        lane < row, shared, jnp.where(lane == row, diagonal, other)
    )


def factors(done_ref, start, width):
    row = iota((width, width), 0)
    lane = iota((width, width), 1)
    whole = jnp.concatenate([done_ref[t, start : start + width, :] for t in range(2)], 1)
    upper = jnp.where(lane > row, whole, jnp.where(lane == row, 1.0 / whole, 0.0))
    return upper, jnp.where(lane <= row, whole, 0.0)


def pair_kernel(
    sample_ref,
    leaf_ref,
    near_ref,
    basis_ref,
    transfer_ref,
    upper_ref,
    pair_ref,
    tile_ref,
    done_ref,
):
    width = sample_ref.shape[0]
    leaf = leaf_ref[...]
    pair = leaf + near_ref[...]
    pair_ref[...] = pair
    unpack(leaf, tile_ref, 0, width)
    unpack(pair, tile_ref, width, width)
    eliminate(tile_ref, done_ref, 2, width)
    leaf_upper, leaf_inverse = factors(done_ref, 0, width)
    upper_ref[...], pair_inverse = factors(done_ref, width, width)
    basis_ref[...] = times_transpose(sample_ref[...].T, leaf_inverse)
    transfer_ref[...] = times_transpose(leaf_upper, pair_inverse)


def group_kernel(
    place_ref,
    pair_ref,
    far_ref,
    last_ref,
    pair_upper_ref,
    transfer_ref,
    factor_ref,
    tile_ref,
    done_ref,
    upper_ref,
):
    width = pair_upper_ref.shape[0]
    unpack(pair_ref[...] + (far_ref[...] + last_ref[...]), tile_ref, 0, width)
    eliminate(tile_ref, done_ref, 1, width)
    upper_ref[...], inverse = factors(done_ref, 0, width)
    half = width // 2
    quarter = width // 4
    place = place_ref[0]
    pair_upper = pair_upper_ref[pl.ds(pl.multiple_of(place % 2 * half, half), half), :]
    transfer_ref[...] = times_transpose(pair_upper, inverse)
    factor_ref[...] = upper_ref[
        pl.ds(pl.multiple_of(place % 4 * quarter, quarter), quarter), :
    ]


def scratch(problems, width):
    tiles = width // LANES
    return [pltpu.VMEM((tiles, problems * width, LANES), jnp.float32)] * 2


def pair_factors(sample_t, leaf, near):
    width, rows = sample_t.shape
    shapes = [(rows, width), (width, width), (width, width), leaf.shape]
    return pl.pallas_call(
        pair_kernel,
        out_shape=[jax.ShapeDtypeStruct(shape, jnp.float32) for shape in shapes],
        scratch_shapes=scratch(2, width),
        compiler_params=pltpu.CompilerParams(vmem_limit_bytes=24 << 20),
        name="pair",
    )(sample_t, leaf, near)


def group_factors(place, pair, far, last, pair_upper):
    width = pair_upper.shape[0]
    shapes = [(width // 2, width), (width // 4, width)]
    return pl.pallas_call(
        group_kernel,
        out_shape=[jax.ShapeDtypeStruct(shape, jnp.float32) for shape in shapes],
        in_specs=[pl.BlockSpec(memory_space=pltpu.SMEM)]
        + [pl.BlockSpec(memory_space=pltpu.VMEM)] * 4,
        scratch_shapes=scratch(1, width) + [pltpu.VMEM((width, width), jnp.float32)],
        compiler_params=pltpu.CompilerParams(vmem_limit_bytes=24 << 20),
        name="group",
    )(place, pair, far, last, pair_upper)


def local(probes, spectrum):
    devices = lax.axis_size("row") * lax.axis_size("col")
    axes = ("row", "col")
    columns = lax.all_to_all(
        spread(probes, spectrum, devices), axes, split_axis=0, concat_axis=0, tiled=True
    )
    moved = circulant(columns, probes.shape[0], devices)
    sample_t = lax.all_to_all(moved, axes, split_axis=0, concat_axis=0, tiled=True)
    leaf = packed_gram(sample_t)
    near, far, last = (partner(leaf, "col", mask) for mask in (1, 2, 3))
    leaf_basis, leaf_transfer, pair_upper, pair = pair_factors(sample_t, leaf, near)
    place = lax.axis_index("col").reshape(1).astype(jnp.int32)
    pair_transfer, group_factor = group_factors(place, pair, far, last, pair_upper)
    return leaf_basis, leaf_transfer, pair_transfer, group_factor


def solution(mesh):
    placed = P(("row", "col"), None)
    return jax.shard_map(
        local,
        mesh=mesh,
        in_specs=(placed, placed),
        out_specs=(placed, placed, placed, placed),
        check_vma=False,
    )
```

```python
import math

import jax
import jax.numpy as jnp
import numpy as np
from jax import lax
from jax.experimental import pallas as pl
from jax.experimental.pallas import tpu as pltpu
from jax.sharding import PartitionSpec as P

LANES = 128
HIGHEST = lax.Precision.HIGHEST


def partner(value, axis, mask):
    pairs = [(source, source ^ mask) for source in range(lax.axis_size(axis))]
    return lax.ppermute(value, axis, pairs)


def matmul(left, right):
    return jnp.dot(left, right, precision=HIGHEST, preferred_element_type=jnp.float32)


def circle(product, length):
    angle = 2.0 * np.pi / length * (product % length)
    return np.cos(angle), np.sin(angle)


def halves(table):
    high = table.astype(jnp.bfloat16)
    return np.stack([high, (table - high.astype(np.float64)).astype(jnp.bfloat16)])


def split2(value):
    high = value.astype(jnp.bfloat16)
    return high, (value - high.astype(jnp.float32)).astype(jnp.bfloat16)


def product(left, right):
    def dot(i, j):
        return jnp.dot(left[i], right[j], preferred_element_type=jnp.float32)

    return dot(0, 0) + (dot(0, 1) + dot(1, 0))


def tables(devices, split):
    major = devices * split
    total = major * LANES
    order = (np.arange(devices)[None, :] * split + np.arange(split)[:, None]).reshape(-1)
    freq = np.arange(major)
    cos, sin = circle(freq[:, None] * order[None, :], major)
    first = np.block([[cos, sin], [-sin, cos]])
    lane = np.arange(LANES)
    cos, sin = circle(lane[:, None] * lane[None, :], LANES)
    second = np.block([[cos, -sin], [sin, cos]])
    cos_turn, sin_turn = circle(freq[:, None] * lane[None, :], total)
    turn = np.stack([cos_turn, sin_turn])
    return [halves(t) for t in (first, first.T, second, second.T)] + [turn.astype(np.float32)]


def iota(shape, dim):
    return lax.broadcasted_iota(jnp.int32, shape, dim)


def times_transpose(left, right):
    return lax.dot_general(
        left,
        right,
        (((1,), (1,)), ((), ())),
        precision=HIGHEST,
        preferred_element_type=jnp.float32,
    )


def spread_kernel(per_dev, extra):
    def body(probes_ref, spectrum_ref, o_ref):
        rows, width = probes_ref.shape
        split = rows // LANES
        for j in range(split):
            lanes = slice(j * LANES, (j + 1) * LANES)
            o_ref[:, lanes] = probes_ref[lanes, :].T
        place = iota((LANES, rows), 1)
        own = jnp.where(place // split == iota((LANES, rows), 0), spectrum_ref[...], 0.0)
        for t in range(extra):
            part = iota((8, rows), 0) % per_dev + t * per_dev
            pick = jnp.where(iota((8, rows), 1) % split == part, 1.0, 0.0)
            symbol = times_transpose(pick, own)
            for r in range(0, width, 8):
                o_ref[r : r + 8, rows + t * LANES : rows + (t + 1) * LANES] = symbol

    return body


def spread(probes, spectrum, devices):
    rows, width = probes.shape
    per_dev = width // devices
    extra = pl.cdiv(rows // LANES, per_dev)
    return pl.pallas_call(
        spread_kernel(per_dev, extra),
        out_shape=jax.ShapeDtypeStruct((width, rows + extra * LANES), jnp.float32),
        name="spread",
    )(probes, spectrum)


def circulant_kernel(devices, split, per_dev, extra):
    major = devices * split
    pairs = per_dev // 2
    width = devices * per_dev

    def symmetric_symbol(tile_ref):
        lam = jnp.concatenate(
            [
                tile_ref[
                    pl.ds((split + h // per_dev) * width + h % per_dev, devices, stride=per_dev), :
                ]
                for h in range(split)
            ],
            0,
        )
        row = iota((LANES, LANES), 0)
        lane = iota((LANES, LANES), 1)
        flip = jnp.where(row + lane == LANES - 1, 1.0, 0.0)
        head_flip = jnp.where((row + lane) % LANES == 0, 1.0, 0.0)
        back = matmul(lam, jnp.concatenate([flip, head_flip], 1))
        row = iota((major, major), 0)
        lane = iota((major, major), 1)
        turn = jnp.where(row + lane == major, 1.0, 0.0)
        other = jnp.where(
            iota((major, LANES), 0) == 0, back[:, LANES:], matmul(turn, back[:, :LANES])
        )
        return (lam + other) * (0.5 / (major * LANES))

    def body(x_ref, first_ref, first_t_ref, second_ref, second_t_ref, turn_ref, o_ref, tile_ref):
        cos = turn_ref[0]
        sin = turn_ref[1]
        for j in range(split + extra):
            tile_ref[j * width : (j + 1) * width, :] = x_ref[:, j * LANES : (j + 1) * LANES]
        lam = symmetric_symbol(tile_ref)

        def column(c):
            return [
                tile_ref[pl.ds(j * width + c, devices, stride=per_dev), :] for j in range(split)
            ]

        packed = jnp.concatenate(
            [jnp.concatenate(column(2 * q) + column(2 * q + 1), 0) for q in range(pairs)], 1
        )
        mixed = product(first_ref, split2(packed))
        turned = []
        for q in range(pairs):
            real = mixed[:major, q * LANES : (q + 1) * LANES]
            imag = mixed[major:, q * LANES : (q + 1) * LANES]
            turned.append(
                jnp.concatenate([real * cos + imag * sin, imag * cos - real * sin], 1)
            )
        spectra = product(split2(jnp.concatenate(turned, 0)), second_ref)
        lam = jnp.concatenate([lam, lam], 1)
        spectra = jnp.concatenate(
            [spectra[q * major : (q + 1) * major] * lam for q in range(pairs)], 0
        )
        back = product(split2(spectra), second_t_ref)
        turned = []
        for q in range(pairs):
            real = back[q * major : (q + 1) * major, :LANES]
            imag = back[q * major : (q + 1) * major, LANES:]
            turned.append(
                jnp.concatenate([real * cos - imag * sin, imag * cos + real * sin], 0)
            )
        sample = product(first_t_ref, split2(jnp.concatenate(turned, 1)))
        for c in range(per_dev):
            for j in range(split):
                row = (c % 2) * major + j * devices
                lane = (c // 2) * LANES
                tile_ref[pl.ds(j * width + c, devices, stride=per_dev), :] = sample[
                    row : row + devices, lane : lane + LANES
                ]
        for j in range(split):
            o_ref[:, j * LANES : (j + 1) * LANES] = tile_ref[j * width : (j + 1) * width, :]

    return body


def circulant(columns, rows, devices):
    width = columns.shape[0]
    split = rows // LANES
    tiles = columns.shape[1] // LANES
    return pl.pallas_call(
        circulant_kernel(devices, split, width // devices, tiles - split),
        out_shape=jax.ShapeDtypeStruct((width, rows), jnp.float32),
        scratch_shapes=[pltpu.VMEM((tiles * width, LANES), jnp.float32)],
        compiler_params=pltpu.CompilerParams(vmem_limit_bytes=48 << 20),
        name="circulant",
    )(columns, *tables(devices, split))


def packed_gram(sample_t):
    gram = times_transpose(sample_t, sample_t) * (1.0 / sample_t.shape[1])
    row = iota((LANES, LANES), 0)
    lane = iota((LANES, LANES), 1)
    last = gram[LANES:, LANES:]
    shared = jnp.where(lane >= row, gram[:LANES, :LANES], last)
    diagonal = jnp.sum(jnp.where(lane == row, last, 0.0), axis=0, keepdims=True)
    return jnp.concatenate(
        [shared, gram[:LANES, LANES:], jnp.broadcast_to(diagonal, (8, LANES))], 0
    )


def parts(value):
    high = value.astype(jnp.bfloat16).astype(jnp.float32)
    rest = value - high
    middle = rest.astype(jnp.bfloat16).astype(jnp.float32)
    return high, middle, rest - middle


def eliminate(tile_ref, done_ref, problems, width):
    tiles = width // LANES
    block = 8
    shape = (block, LANES)
    sub = iota(shape, 0)
    lane = iota(shape, 1)

    def row_of(value, i):
        return jnp.broadcast_to(value[i : i + 1, :], shape)

    def lane_of(value, l):
        return jnp.broadcast_to(value[:, l : l + 1], shape)

    def turned(value, l):
        only = jnp.sum(jnp.where(lane == sub + l, value, 0.0), axis=1, keepdims=True)
        return jnp.broadcast_to(only, shape)

    def load(base):
        return [
            [
                tile_ref[t, p * width + base : p * width + base + block, :]
                for t in range(tiles)
            ]
            for p in range(problems)
        ]

    panel = load(0)
    for base in range(0, width, block):
        own, offset = divmod(base, LANES)
        after = base + block
        more = after < width
        column = [[lane_of(x[own], offset + l) for l in range(block)] for x in panel]
        inside = (lane >= offset) & (lane < offset + block)
        if more:
            near, shift = divmod(after, LANES)
            cross = [[turned(row_of(x[near], i), shift) for i in range(block)] for x in panel]
            ahead = load(after)
            for x in ahead:
                x[own] = jnp.where(inside, 0.0, x[own])
        for j in range(block):
            hot = (lane == offset + j) & (sub >= j)
            unit = jnp.where(sub == j, 1.0, 0.0)
            for p in range(problems):
                x, c = panel[p], column[p]
                scale = lax.rsqrt(row_of(c[j], j))
                factor = c[j] * scale
                each = {l: row_of(factor, l) for l in range(j + 1, block)}
                for l in range(j + 1, block):
                    c[l] = c[l] - factor * each[l]
                lower = jnp.where(sub > j, factor, 0.0)
                x[own] = jnp.where(hot, unit, x[own])
                pivot = [row_of(y, j) * scale for y in x]
                panel[p] = [
                    jnp.where(sub == j, v, y - lower * v) for v, y in zip(pivot, x)
                ]
                if more:
                    weight = cross[p][j] * scale
                    for i in range(j + 1, block):
                        cross[p][i] = cross[p][i] - each[i] * weight
                    pivot[own] = jnp.where(inside & (lane > offset + j), 0.0, pivot[own])
                    ahead[p] = [y - weight * v for v, y in zip(pivot, ahead[p])]
        for p in range(problems):
            for t in range(tiles):
                done_ref[t, p * width + base : p * width + after, :] = panel[p][t]
        if not more:
            break
        done, panel = panel, ahead
        past = after + block
        if past == width:
            continue
        first = past // LANES
        inverse = ~inside | (lane - offset <= sub)
        below = iota((width - past, LANES), 1) - offset
        below = (below >= 0) & (below < block)
        for p in range(problems):
            start = p * width
            rows = [parts(x) for x in done[p]]
            left = jnp.concatenate(
                [
                    jnp.concatenate([rows[t][q] for q in (0, 0, 1, 1, 0, 2)], 0)
                    for t in range(first, tiles)
                ],
                1,
            ).astype(jnp.bfloat16)
            rows[own] = [jnp.where(inverse, x, 0.0) for x in rows[own]]
            right = jnp.concatenate(
                [
                    jnp.concatenate([rows[t][q] for q in (0, 1, 0, 1, 2, 0)], 0)
                    for t in range(tiles)
                ],
                1,
            ).astype(jnp.bfloat16)
            update = lax.dot_general(
                left, right, (((0,), (0,)), ((), ())), preferred_element_type=jnp.float32
            )
            for t in range(tiles):
                old = tile_ref[t, start + past : start + width, :]
                if t == own:
                    old = jnp.where(below, 0.0, old)
                tile_ref[t, start + past : start + width, :] = (
                    old - update[past - first * LANES :, t * LANES : (t + 1) * LANES]
                )


def unpack(packed, tile_ref, start, width):
    row = iota((LANES, LANES), 0)
    lane = iota((LANES, LANES), 1)
    shared = packed[:LANES, :]
    other = shared.T
    tile_ref[0, start : start + LANES, :] = jnp.where(lane >= row, shared, other)
    tile_ref[0, start + LANES : start + width, :] = jnp.zeros((LANES, LANES), jnp.float32)
    tile_ref[1, start : start + LANES, :] = packed[LANES : 2 * LANES, :]
    diagonal = jnp.broadcast_to(packed[2 * LANES : 2 * LANES + 1, :], (LANES, LANES))
    tile_ref[1, start + LANES : start + width, :] = jnp.where(
        lane < row, shared, jnp.where(lane == row, diagonal, other)
    )


def factors(done_ref, start, width):
    row = iota((width, width), 0)
    lane = iota((width, width), 1)
    whole = jnp.concatenate([done_ref[t, start : start + width, :] for t in range(2)], 1)
    upper = jnp.where(lane > row, whole, jnp.where(lane == row, 1.0 / whole, 0.0))
    return upper, jnp.where(lane <= row, whole, 0.0)


def leaf_kernel(sample_ref, packed_ref, basis_ref, upper_ref, tile_ref, done_ref):
    width = sample_ref.shape[0]
    unpack(packed_ref[...], tile_ref, 0, width)
    eliminate(tile_ref, done_ref, 1, width)
    upper, inverse = factors(done_ref, 0, width)
    upper_ref[...] = upper
    basis_ref[...] = times_transpose(sample_ref[...].T, inverse)


def group_kernel(
    place_ref,
    leaf_ref,
    near_ref,
    far_ref,
    last_ref,
    leaf_upper_ref,
    leaf_transfer_ref,
    pair_transfer_ref,
    group_factor_ref,
    tile_ref,
    done_ref,
    upper_ref,
):
    width = leaf_upper_ref.shape[0]
    pair = leaf_ref[...] + near_ref[...]
    unpack(pair, tile_ref, 0, width)
    unpack(pair + (far_ref[...] + last_ref[...]), tile_ref, width, width)
    eliminate(tile_ref, done_ref, 2, width)
    upper_ref[0], pair_inverse = factors(done_ref, 0, width)
    upper_ref[1], group_inverse = factors(done_ref, width, width)
    leaf_transfer_ref[...] = times_transpose(leaf_upper_ref[...], pair_inverse)
    half = width // 2
    quarter = width // 4
    place = place_ref[0]
    pair_upper = upper_ref[0, pl.ds(pl.multiple_of(place % 2 * half, half), half), :]
    pair_transfer_ref[...] = times_transpose(pair_upper, group_inverse)
    group_factor_ref[...] = upper_ref[
        1, pl.ds(pl.multiple_of(place % 4 * quarter, quarter), quarter), :
    ]


def scratch(problems, width):
    tiles = width // LANES
    return [pltpu.VMEM((tiles, problems * width, LANES), jnp.float32)] * 2


def leaf_factor(sample_t, leaf):
    width, rows = sample_t.shape
    return pl.pallas_call(
        leaf_kernel,
        out_shape=[jax.ShapeDtypeStruct(shape, jnp.float32) for shape in ((rows, width), (width, width))],
        scratch_shapes=scratch(1, width),
        compiler_params=pltpu.CompilerParams(vmem_limit_bytes=24 << 20),
        name="leaf",
    )(sample_t, leaf)


def group_factors(place, leaf, near, far, last, leaf_upper):
    width = leaf_upper.shape[0]
    shapes = [(width, width), (width // 2, width), (width // 4, width)]
    return pl.pallas_call(
        group_kernel,
        out_shape=[jax.ShapeDtypeStruct(shape, jnp.float32) for shape in shapes],
        in_specs=[pl.BlockSpec(memory_space=pltpu.SMEM)]
        + [pl.BlockSpec(memory_space=pltpu.VMEM)] * 5,
        scratch_shapes=scratch(2, width) + [pltpu.VMEM((2, width, width), jnp.float32)],
        compiler_params=pltpu.CompilerParams(vmem_limit_bytes=24 << 20),
        name="group",
    )(place, leaf, near, far, last, leaf_upper)


def local(probes, spectrum):
    devices = lax.axis_size("row") * lax.axis_size("col")
    axes = ("row", "col")
    columns = lax.all_to_all(
        spread(probes, spectrum, devices), axes, split_axis=0, concat_axis=0, tiled=True
    )
    moved = circulant(columns, probes.shape[0], devices)
    sample_t = lax.all_to_all(moved, axes, split_axis=0, concat_axis=0, tiled=True)
    leaf = packed_gram(sample_t)
    far, last, near = (partner(leaf, "col", mask) for mask in (2, 3, 1))
    leaf_basis, leaf_upper = leaf_factor(sample_t, leaf)
    place = lax.axis_index("col").reshape(1).astype(jnp.int32)
    return (leaf_basis, *group_factors(place, leaf, near, far, last, leaf_upper))


def solution(mesh):
    placed = P(("row", "col"), None)
    return jax.shard_map(
        local,
        mesh=mesh,
        in_specs=(placed, placed),
        out_specs=(placed, placed, placed, placed),
        check_vma=False,
    )
```

```python
import math

import jax
import jax.numpy as jnp
import numpy as np
from jax import lax
from jax.experimental import pallas as pl
from jax.experimental.pallas import tpu as pltpu
from jax.sharding import PartitionSpec as P

LANES = 128
HIGHEST = lax.Precision.HIGHEST


def partner(value, axis, mask):
    pairs = [(source, source ^ mask) for source in range(lax.axis_size(axis))]
    return lax.ppermute(value, axis, pairs)


def matmul(left, right):
    return jnp.dot(left, right, precision=HIGHEST, preferred_element_type=jnp.float32)


def circle(product, length):
    angle = 2.0 * np.pi / length * (product % length)
    return np.cos(angle), np.sin(angle)


def halves(table):
    high = table.astype(jnp.bfloat16)
    return np.stack([high, (table - high.astype(np.float64)).astype(jnp.bfloat16)])


def split2(value):
    high = value.astype(jnp.bfloat16)
    return high, (value - high.astype(jnp.float32)).astype(jnp.bfloat16)


def product(left, right):
    def dot(i, j):
        return jnp.dot(left[i], right[j], preferred_element_type=jnp.float32)

    return dot(0, 0) + (dot(0, 1) + dot(1, 0))


def tables(devices, split):
    major = devices * split
    total = major * LANES
    order = (np.arange(devices)[None, :] * split + np.arange(split)[:, None]).reshape(-1)
    freq = np.arange(major)
    cos, sin = circle(freq[:, None] * order[None, :], major)
    first = np.block([[cos, sin], [-sin, cos]])
    lane = np.arange(LANES)
    cos, sin = circle(lane[:, None] * lane[None, :], LANES)
    second = np.block([[cos, -sin], [sin, cos]])
    cos_turn, sin_turn = circle(freq[:, None] * lane[None, :], total)
    turn = np.stack([cos_turn, sin_turn])
    return [halves(t) for t in (first, first.T, second, second.T)] + [turn.astype(np.float32)]


def iota(shape, dim):
    return lax.broadcasted_iota(jnp.int32, shape, dim)


def times_transpose(left, right):
    return lax.dot_general(
        left,
        right,
        (((1,), (1,)), ((), ())),
        precision=HIGHEST,
        preferred_element_type=jnp.float32,
    )


def spread_kernel(per_dev, extra):
    def body(probes_ref, spectrum_ref, o_ref):
        rows, width = probes_ref.shape
        split = rows // LANES
        for j in range(split):
            lanes = slice(j * LANES, (j + 1) * LANES)
            o_ref[:, lanes] = probes_ref[lanes, :].T
        place = iota((LANES, rows), 1)
        own = jnp.where(place // split == iota((LANES, rows), 0), spectrum_ref[...], 0.0)
        for t in range(extra):
            part = iota((8, rows), 0) % per_dev + t * per_dev
            pick = jnp.where(iota((8, rows), 1) % split == part, 1.0, 0.0)
            symbol = times_transpose(pick, own)
            for r in range(0, width, 8):
                o_ref[r : r + 8, rows + t * LANES : rows + (t + 1) * LANES] = symbol

    return body


def spread(probes, spectrum, devices):
    rows, width = probes.shape
    per_dev = width // devices
    extra = pl.cdiv(rows // LANES, per_dev)
    return pl.pallas_call(
        spread_kernel(per_dev, extra),
        out_shape=jax.ShapeDtypeStruct((width, rows + extra * LANES), jnp.float32),
        name="spread",
    )(probes, spectrum)


def circulant_kernel(devices, split, per_dev, extra):
    major = devices * split
    pairs = per_dev // 2
    width = devices * per_dev

    def symmetric_symbol(tile_ref):
        lam = jnp.concatenate(
            [
                tile_ref[
                    pl.ds((split + h // per_dev) * width + h % per_dev, devices, stride=per_dev), :
                ]
                for h in range(split)
            ],
            0,
        )
        row = iota((LANES, LANES), 0)
        lane = iota((LANES, LANES), 1)
        flip = jnp.where(row + lane == LANES - 1, 1.0, 0.0)
        head_flip = jnp.where((row + lane) % LANES == 0, 1.0, 0.0)
        back = matmul(lam, jnp.concatenate([flip, head_flip], 1))
        row = iota((major, major), 0)
        lane = iota((major, major), 1)
        turn = jnp.where(row + lane == major, 1.0, 0.0)
        other = jnp.where(
            iota((major, LANES), 0) == 0, back[:, LANES:], matmul(turn, back[:, :LANES])
        )
        return (lam + other) * (0.5 / (major * LANES))

    def body(x_ref, first_ref, first_t_ref, second_ref, second_t_ref, turn_ref, o_ref, tile_ref):
        cos = turn_ref[0]
        sin = turn_ref[1]
        for j in range(split + extra):
            tile_ref[j * width : (j + 1) * width, :] = x_ref[:, j * LANES : (j + 1) * LANES]
        lam = symmetric_symbol(tile_ref)

        def column(c):
            return [
                tile_ref[pl.ds(j * width + c, devices, stride=per_dev), :] for j in range(split)
            ]

        packed = jnp.concatenate(
            [jnp.concatenate(column(2 * q) + column(2 * q + 1), 0) for q in range(pairs)], 1
        )
        mixed = product(first_ref, split2(packed))
        turned = []
        for q in range(pairs):
            real = mixed[:major, q * LANES : (q + 1) * LANES]
            imag = mixed[major:, q * LANES : (q + 1) * LANES]
            turned.append(
                jnp.concatenate([real * cos + imag * sin, imag * cos - real * sin], 1)
            )
        spectra = product(split2(jnp.concatenate(turned, 0)), second_ref)
        lam = jnp.concatenate([lam, lam], 1)
        spectra = jnp.concatenate(
            [spectra[q * major : (q + 1) * major] * lam for q in range(pairs)], 0
        )
        back = product(split2(spectra), second_t_ref)
        turned = []
        for q in range(pairs):
            real = back[q * major : (q + 1) * major, :LANES]
            imag = back[q * major : (q + 1) * major, LANES:]
            turned.append(
                jnp.concatenate([real * cos - imag * sin, imag * cos + real * sin], 0)
            )
        sample = product(first_t_ref, split2(jnp.concatenate(turned, 1)))
        for c in range(per_dev):
            for j in range(split):
                row = (c % 2) * major + j * devices
                lane = (c // 2) * LANES
                tile_ref[pl.ds(j * width + c, devices, stride=per_dev), :] = sample[
                    row : row + devices, lane : lane + LANES
                ]
        for j in range(split):
            o_ref[:, j * LANES : (j + 1) * LANES] = tile_ref[j * width : (j + 1) * width, :]

    return body


def circulant(columns, rows, devices):
    width = columns.shape[0]
    split = rows // LANES
    tiles = columns.shape[1] // LANES
    return pl.pallas_call(
        circulant_kernel(devices, split, width // devices, tiles - split),
        out_shape=jax.ShapeDtypeStruct((width, rows), jnp.float32),
        scratch_shapes=[pltpu.VMEM((tiles * width, LANES), jnp.float32)],
        compiler_params=pltpu.CompilerParams(vmem_limit_bytes=48 << 20),
        name="circulant",
    )(columns, *tables(devices, split))


def packed_gram(sample_t):
    gram = times_transpose(sample_t, sample_t) * (1.0 / sample_t.shape[1])
    row = iota((LANES, LANES), 0)
    lane = iota((LANES, LANES), 1)
    last = gram[LANES:, LANES:]
    shared = jnp.where(lane >= row, gram[:LANES, :LANES], last)
    diagonal = jnp.sum(jnp.where(lane == row, last, 0.0), axis=0, keepdims=True)
    return jnp.concatenate(
        [shared, gram[:LANES, LANES:], jnp.broadcast_to(diagonal, (8, LANES))], 0
    )


def parts(value):
    high = value.astype(jnp.bfloat16).astype(jnp.float32)
    rest = value - high
    middle = rest.astype(jnp.bfloat16).astype(jnp.float32)
    return high, middle, rest - middle


def eliminate(tile_ref, done_ref, problems, width):
    tiles = width // LANES
    block = 8
    shape = (block, LANES)
    sub = iota(shape, 0)
    lane = iota(shape, 1)

    def row_of(value, i):
        return jnp.broadcast_to(value[i : i + 1, :], shape)

    def lane_of(value, l):
        return jnp.broadcast_to(value[:, l : l + 1], shape)

    def turned(value, l):
        only = jnp.sum(jnp.where(lane == sub + l, value, 0.0), axis=1, keepdims=True)
        return jnp.broadcast_to(only, shape)

    def load(base):
        return [
            [
                tile_ref[t, p * width + base : p * width + base + block, :]
                for t in range(tiles)
            ]
            for p in range(problems)
        ]

    def stack(rows, order):
        return jnp.concatenate(
            [jnp.concatenate([row[q] for q in order], 0) for row in rows], 1
        ).astype(jnp.bfloat16)

    def outer(left, right):
        return lax.dot_general(
            left, right, (((0,), (0,)), ((), ())), preferred_element_type=jnp.float32
        )

    def defer(begin, end):
        keep = iota((end - begin, LANES), 1) <= iota((end - begin, LANES), 0) + begin
        for p in range(problems):
            start = p * width
            rows = [parts(done_ref[t, start + begin : start + end, :]) for t in range(tiles)]
            left = stack(rows[1:], (0, 0, 1, 1, 0, 2))
            rows[0] = [jnp.where(keep, x, 0.0) for x in rows[0]]
            update = outer(left, stack(rows, (0, 1, 0, 1, 2, 0)))
            for t in range(tiles):
                tile_ref[t, start + LANES : start + width, :] = (
                    tile_ref[t, start + LANES : start + width, :]
                    - update[:, t * LANES : (t + 1) * LANES]
                )

    panel = load(0)
    for base in range(0, width, block):
        own, offset = divmod(base, LANES)
        after = base + block
        more = after < width
        column = [[lane_of(x[own], offset + l) for l in range(block)] for x in panel]
        inside = (lane >= offset) & (lane < offset + block)
        if more:
            near, shift = divmod(after, LANES)
            cross = [[turned(row_of(x[near], i), shift) for i in range(block)] for x in panel]
            ahead = load(after)
            for x in ahead:
                x[own] = jnp.where(inside, 0.0, x[own])
        for j in range(block):
            hot = (lane == offset + j) & (sub >= j)
            unit = jnp.where(sub == j, 1.0, 0.0)
            for p in range(problems):
                x, c = panel[p], column[p]
                scale = lax.rsqrt(row_of(c[j], j))
                factor = c[j] * scale
                each = {l: row_of(factor, l) for l in range(j + 1, block)}
                for l in range(j + 1, block):
                    c[l] = c[l] - factor * each[l]
                lower = jnp.where(sub > j, factor, 0.0)
                x[own] = jnp.where(hot, unit, x[own])
                pivot = [row_of(y, j) * scale for y in x]
                panel[p] = [
                    jnp.where(sub == j, v, y - lower * v) for v, y in zip(pivot, x)
                ]
                if more:
                    weight = cross[p][j] * scale
                    for i in range(j + 1, block):
                        cross[p][i] = cross[p][i] - each[i] * weight
                    pivot[own] = jnp.where(inside & (lane > offset + j), 0.0, pivot[own])
                    ahead[p] = [y - weight * v for v, y in zip(pivot, ahead[p])]
        for p in range(problems):
            for t in range(tiles):
                done_ref[t, p * width + base : p * width + after, :] = panel[p][t]
        if not more:
            break
        done, panel = panel, ahead
        if base == LANES // 2 - block:
            defer(0, LANES // 2)
        if base == LANES - 2 * block:
            defer(LANES // 2, LANES - block)
        past = after + block
        stop = LANES if after < LANES else width
        if past >= stop:
            continue
        first = past // LANES
        inverse = ~inside | (lane - offset <= sub)
        below = iota((stop - past, LANES), 1) - offset
        below = (below >= 0) & (below < block)
        for p in range(problems):
            start = p * width
            rows = [parts(x) for x in done[p]]
            left = stack(rows[first : pl.cdiv(stop, LANES)], (0, 0, 1, 1, 0, 2))
            rows[own] = [jnp.where(inverse, x, 0.0) for x in rows[own]]
            update = outer(left, stack(rows, (0, 1, 0, 1, 2, 0)))
            for t in range(tiles):
                old = tile_ref[t, start + past : start + stop, :]
                if t == own:
                    old = jnp.where(below, 0.0, old)
                tile_ref[t, start + past : start + stop, :] = (
                    old
                    - update[past - first * LANES : stop - first * LANES, t * LANES : (t + 1) * LANES]
                )


def unpack(packed, tile_ref, start, width):
    row = iota((LANES, LANES), 0)
    lane = iota((LANES, LANES), 1)
    shared = packed[:LANES, :]
    other = shared.T
    tile_ref[0, start : start + LANES, :] = jnp.where(lane >= row, shared, other)
    tile_ref[0, start + LANES : start + width, :] = jnp.zeros((LANES, LANES), jnp.float32)
    tile_ref[1, start : start + LANES, :] = packed[LANES : 2 * LANES, :]
    diagonal = jnp.broadcast_to(packed[2 * LANES : 2 * LANES + 1, :], (LANES, LANES))
    tile_ref[1, start + LANES : start + width, :] = jnp.where(
        lane < row, shared, jnp.where(lane == row, diagonal, other)
    )


def factors(done_ref, start, width):
    row = iota((width, width), 0)
    lane = iota((width, width), 1)
    whole = jnp.concatenate([done_ref[t, start : start + width, :] for t in range(2)], 1)
    upper = jnp.where(lane > row, whole, jnp.where(lane == row, 1.0 / whole, 0.0))
    return upper, jnp.where(lane <= row, whole, 0.0)


def leaf_kernel(sample_ref, packed_ref, basis_ref, upper_ref, tile_ref, done_ref):
    width = sample_ref.shape[0]
    unpack(packed_ref[...], tile_ref, 0, width)
    eliminate(tile_ref, done_ref, 1, width)
    upper, inverse = factors(done_ref, 0, width)
    upper_ref[...] = upper
    basis_ref[...] = times_transpose(sample_ref[...].T, inverse)


def group_kernel(
    place_ref,
    leaf_ref,
    near_ref,
    far_ref,
    last_ref,
    leaf_upper_ref,
    leaf_transfer_ref,
    pair_transfer_ref,
    group_factor_ref,
    tile_ref,
    done_ref,
    upper_ref,
):
    width = leaf_upper_ref.shape[0]
    pair = leaf_ref[...] + near_ref[...]
    unpack(pair, tile_ref, 0, width)
    unpack(pair + (far_ref[...] + last_ref[...]), tile_ref, width, width)
    eliminate(tile_ref, done_ref, 2, width)
    upper_ref[0], pair_inverse = factors(done_ref, 0, width)
    upper_ref[1], group_inverse = factors(done_ref, width, width)
    leaf_transfer_ref[...] = times_transpose(leaf_upper_ref[...], pair_inverse)
    half = width // 2
    quarter = width // 4
    place = place_ref[0]
    pair_upper = upper_ref[0, pl.ds(pl.multiple_of(place % 2 * half, half), half), :]
    pair_transfer_ref[...] = times_transpose(pair_upper, group_inverse)
    group_factor_ref[...] = upper_ref[
        1, pl.ds(pl.multiple_of(place % 4 * quarter, quarter), quarter), :
    ]


def scratch(problems, width):
    tiles = width // LANES
    return [pltpu.VMEM((tiles, problems * width, LANES), jnp.float32)] * 2


def leaf_factor(sample_t, leaf):
    width, rows = sample_t.shape
    return pl.pallas_call(
        leaf_kernel,
        out_shape=[jax.ShapeDtypeStruct(shape, jnp.float32) for shape in ((rows, width), (width, width))],
        scratch_shapes=scratch(1, width),
        compiler_params=pltpu.CompilerParams(vmem_limit_bytes=24 << 20),
        name="leaf",
    )(sample_t, leaf)


def group_factors(place, leaf, near, far, last, leaf_upper):
    width = leaf_upper.shape[0]
    shapes = [(width, width), (width // 2, width), (width // 4, width)]
    return pl.pallas_call(
        group_kernel,
        out_shape=[jax.ShapeDtypeStruct(shape, jnp.float32) for shape in shapes],
        in_specs=[pl.BlockSpec(memory_space=pltpu.SMEM)]
        + [pl.BlockSpec(memory_space=pltpu.VMEM)] * 5,
        scratch_shapes=scratch(2, width) + [pltpu.VMEM((2, width, width), jnp.float32)],
        compiler_params=pltpu.CompilerParams(vmem_limit_bytes=24 << 20),
        name="group",
    )(place, leaf, near, far, last, leaf_upper)


def local(probes, spectrum):
    devices = lax.axis_size("row") * lax.axis_size("col")
    axes = ("row", "col")
    columns = lax.all_to_all(
        spread(probes, spectrum, devices), axes, split_axis=0, concat_axis=0, tiled=True
    )
    moved = circulant(columns, probes.shape[0], devices)
    sample_t = lax.all_to_all(moved, axes, split_axis=0, concat_axis=0, tiled=True)
    leaf = packed_gram(sample_t)
    far, last, near = (partner(leaf, "col", mask) for mask in (2, 3, 1))
    leaf_basis, leaf_upper = leaf_factor(sample_t, leaf)
    place = lax.axis_index("col").reshape(1).astype(jnp.int32)
    return (leaf_basis, *group_factors(place, leaf, near, far, last, leaf_upper))


def solution(mesh):
    placed = P(("row", "col"), None)
    return jax.shard_map(
        local,
        mesh=mesh,
        in_specs=(placed, placed),
        out_specs=(placed, placed, placed, placed),
        check_vma=False,
    )
```

```python
import math

import jax
import jax.numpy as jnp
import numpy as np
from jax import lax
from jax.experimental import pallas as pl
from jax.experimental.pallas import tpu as pltpu
from jax.sharding import PartitionSpec as P

LANES = 128
HIGHEST = lax.Precision.HIGHEST


def partner(value, axis, mask):
    pairs = [(source, source ^ mask) for source in range(lax.axis_size(axis))]
    return lax.ppermute(value, axis, pairs)


def matmul(left, right):
    return jnp.dot(left, right, precision=HIGHEST, preferred_element_type=jnp.float32)


def circle(product, length):
    angle = 2.0 * np.pi / length * (product % length)
    return np.cos(angle), np.sin(angle)


def halves(table):
    high = table.astype(jnp.bfloat16)
    return np.stack([high, (table - high.astype(np.float64)).astype(jnp.bfloat16)])


def split2(value):
    high = value.astype(jnp.bfloat16)
    return high, (value - high.astype(jnp.float32)).astype(jnp.bfloat16)


def product(left, right):
    def dot(i, j):
        return jnp.dot(left[i], right[j], preferred_element_type=jnp.float32)

    return dot(0, 0) + (dot(0, 1) + dot(1, 0))


def product_transpose(left, right):
    left, right = split2(left), split2(right)

    def dot(i, j):
        return lax.dot_general(
            left[i], right[j], (((1,), (1,)), ((), ())), preferred_element_type=jnp.float32
        )

    return dot(0, 0) + (dot(0, 1) + dot(1, 0))


def tables(devices, split):
    major = devices * split
    total = major * LANES
    order = (np.arange(devices)[None, :] * split + np.arange(split)[:, None]).reshape(-1)
    freq = np.arange(major)
    cos, sin = circle(freq[:, None] * order[None, :], major)
    first = np.block([[cos, sin], [-sin, cos]])
    lane = np.arange(LANES)
    cos, sin = circle(lane[:, None] * lane[None, :], LANES)
    second = np.block([[cos, -sin], [sin, cos]])
    cos_turn, sin_turn = circle(freq[:, None] * lane[None, :], total)
    turn = np.stack([cos_turn, sin_turn])
    return [halves(t) for t in (first, first.T, second, second.T)] + [turn.astype(np.float32)]


def iota(shape, dim):
    return lax.broadcasted_iota(jnp.int32, shape, dim)


def times_transpose(left, right):
    return lax.dot_general(
        left,
        right,
        (((1,), (1,)), ((), ())),
        precision=HIGHEST,
        preferred_element_type=jnp.float32,
    )


def spread_kernel(per_dev, extra):
    def body(probes_ref, spectrum_ref, o_ref):
        rows, width = probes_ref.shape
        split = rows // LANES
        for j in range(split):
            lanes = slice(j * LANES, (j + 1) * LANES)
            o_ref[:, lanes] = probes_ref[lanes, :].T
        place = iota((LANES, rows), 1)
        own = jnp.where(place // split == iota((LANES, rows), 0), spectrum_ref[...], 0.0)
        for t in range(extra):
            part = iota((8, rows), 0) % per_dev + t * per_dev
            pick = jnp.where(iota((8, rows), 1) % split == part, 1.0, 0.0)
            symbol = times_transpose(pick, own)
            for r in range(0, width, 8):
                o_ref[r : r + 8, rows + t * LANES : rows + (t + 1) * LANES] = symbol

    return body


def spread(probes, spectrum, devices):
    rows, width = probes.shape
    per_dev = width // devices
    extra = pl.cdiv(rows // LANES, per_dev)
    return pl.pallas_call(
        spread_kernel(per_dev, extra),
        out_shape=jax.ShapeDtypeStruct((width, rows + extra * LANES), jnp.float32),
        name="spread",
    )(probes, spectrum)


def circulant_kernel(devices, split, per_dev, extra):
    major = devices * split
    pairs = per_dev // 2
    width = devices * per_dev

    def symmetric_symbol(tile_ref):
        lam = jnp.concatenate(
            [
                tile_ref[
                    pl.ds((split + h // per_dev) * width + h % per_dev, devices, stride=per_dev), :
                ]
                for h in range(split)
            ],
            0,
        )
        row = iota((LANES, LANES), 0)
        lane = iota((LANES, LANES), 1)
        flip = jnp.where(row + lane == LANES - 1, 1.0, 0.0)
        head_flip = jnp.where((row + lane) % LANES == 0, 1.0, 0.0)
        back = matmul(lam, jnp.concatenate([flip, head_flip], 1))
        row = iota((major, major), 0)
        lane = iota((major, major), 1)
        turn = jnp.where(row + lane == major, 1.0, 0.0)
        other = jnp.where(
            iota((major, LANES), 0) == 0, back[:, LANES:], matmul(turn, back[:, :LANES])
        )
        return (lam + other) * (0.5 / (major * LANES))

    def body(x_ref, first_ref, first_t_ref, second_ref, second_t_ref, turn_ref, o_ref, tile_ref):
        cos = turn_ref[0]
        sin = turn_ref[1]
        for j in range(split + extra):
            tile_ref[j * width : (j + 1) * width, :] = x_ref[:, j * LANES : (j + 1) * LANES]
        lam = symmetric_symbol(tile_ref)

        def column(c):
            return [
                tile_ref[pl.ds(j * width + c, devices, stride=per_dev), :] for j in range(split)
            ]

        packed = jnp.concatenate(
            [jnp.concatenate(column(2 * q) + column(2 * q + 1), 0) for q in range(pairs)], 1
        )
        mixed = product(first_ref, split2(packed))
        turned = []
        for q in range(pairs):
            real = mixed[:major, q * LANES : (q + 1) * LANES]
            imag = mixed[major:, q * LANES : (q + 1) * LANES]
            turned.append(
                jnp.concatenate([real * cos + imag * sin, imag * cos - real * sin], 1)
            )
        spectra = product(split2(jnp.concatenate(turned, 0)), second_ref)
        lam = jnp.concatenate([lam, lam], 1)
        spectra = jnp.concatenate(
            [spectra[q * major : (q + 1) * major] * lam for q in range(pairs)], 0
        )
        back = product(split2(spectra), second_t_ref)
        turned = []
        for q in range(pairs):
            real = back[q * major : (q + 1) * major, :LANES]
            imag = back[q * major : (q + 1) * major, LANES:]
            turned.append(
                jnp.concatenate([real * cos - imag * sin, imag * cos + real * sin], 0)
            )
        sample = product(first_t_ref, split2(jnp.concatenate(turned, 1)))
        for c in range(per_dev):
            for j in range(split):
                row = (c % 2) * major + j * devices
                lane = (c // 2) * LANES
                tile_ref[pl.ds(j * width + c, devices, stride=per_dev), :] = sample[
                    row : row + devices, lane : lane + LANES
                ]
        for j in range(split):
            o_ref[:, j * LANES : (j + 1) * LANES] = tile_ref[j * width : (j + 1) * width, :]

    return body


def circulant(columns, rows, devices):
    width = columns.shape[0]
    split = rows // LANES
    tiles = columns.shape[1] // LANES
    return pl.pallas_call(
        circulant_kernel(devices, split, width // devices, tiles - split),
        out_shape=jax.ShapeDtypeStruct((width, rows), jnp.float32),
        scratch_shapes=[pltpu.VMEM((tiles * width, LANES), jnp.float32)],
        compiler_params=pltpu.CompilerParams(vmem_limit_bytes=48 << 20),
        name="circulant",
    )(columns, *tables(devices, split))


def packed_gram(sample_t):
    gram = times_transpose(sample_t, sample_t) * (1.0 / sample_t.shape[1])
    row = iota((LANES, LANES), 0)
    lane = iota((LANES, LANES), 1)
    last = gram[LANES:, LANES:]
    shared = jnp.where(lane >= row, gram[:LANES, :LANES], last)
    diagonal = jnp.sum(jnp.where(lane == row, last, 0.0), axis=0, keepdims=True)
    return jnp.concatenate(
        [shared, gram[:LANES, LANES:], jnp.broadcast_to(diagonal, (8, LANES))], 0
    )


def parts(value):
    high = value.astype(jnp.bfloat16).astype(jnp.float32)
    rest = value - high
    middle = rest.astype(jnp.bfloat16).astype(jnp.float32)
    return high, middle, rest - middle


def eliminate(tile_ref, done_ref, problems, width):
    tiles = width // LANES
    block = 8
    shape = (block, LANES)
    sub = iota(shape, 0)
    lane = iota(shape, 1)

    def row_of(value, i):
        return jnp.broadcast_to(value[i : i + 1, :], shape)

    def lane_of(value, l):
        return jnp.broadcast_to(value[:, l : l + 1], shape)

    def turned(value, l):
        only = jnp.sum(jnp.where(lane == sub + l, value, 0.0), axis=1, keepdims=True)
        return jnp.broadcast_to(only, shape)

    def load(base):
        return [
            [
                tile_ref[t, p * width + base : p * width + base + block, :]
                for t in range(tiles)
            ]
            for p in range(problems)
        ]

    def stack(rows, order):
        return jnp.concatenate(
            [jnp.concatenate([row[q] for q in order], 0) for row in rows], 1
        ).astype(jnp.bfloat16)

    def outer(left, right):
        return lax.dot_general(
            left, right, (((0,), (0,)), ((), ())), preferred_element_type=jnp.float32
        )

    def defer(begin, end):
        keep = iota((end - begin, LANES), 1) <= iota((end - begin, LANES), 0) + begin
        for p in range(problems):
            start = p * width
            rows = [parts(done_ref[t, start + begin : start + end, :]) for t in range(tiles)]
            left = stack(rows[1:], (0, 0, 1, 1, 0, 2))
            rows[0] = [jnp.where(keep, x, 0.0) for x in rows[0]]
            update = outer(left, stack(rows, (0, 1, 0, 1, 2, 0)))
            for t in range(tiles):
                tile_ref[t, start + LANES : start + width, :] = (
                    tile_ref[t, start + LANES : start + width, :]
                    - update[:, t * LANES : (t + 1) * LANES]
                )

    panel = load(0)
    for base in range(0, width, block):
        own, offset = divmod(base, LANES)
        after = base + block
        more = after < width
        column = [[lane_of(x[own], offset + l) for l in range(block)] for x in panel]
        inside = (lane >= offset) & (lane < offset + block)
        if more:
            near, shift = divmod(after, LANES)
            cross = [[turned(row_of(x[near], i), shift) for i in range(block)] for x in panel]
            ahead = load(after)
            for x in ahead:
                x[own] = jnp.where(inside, 0.0, x[own])
        for j in range(block):
            hot = (lane == offset + j) & (sub >= j)
            unit = jnp.where(sub == j, 1.0, 0.0)
            for p in range(problems):
                x, c = panel[p], column[p]
                scale = lax.rsqrt(row_of(c[j], j))
                factor = c[j] * scale
                each = {l: row_of(factor, l) for l in range(j + 1, block)}
                for l in range(j + 1, block):
                    c[l] = c[l] - factor * each[l]
                lower = jnp.where(sub > j, factor, 0.0)
                x[own] = jnp.where(hot, unit, x[own])
                pivot = [row_of(y, j) * scale for y in x]
                panel[p] = [
                    jnp.where(sub == j, v, y - lower * v) for v, y in zip(pivot, x)
                ]
                if more:
                    weight = cross[p][j] * scale
                    for i in range(j + 1, block):
                        cross[p][i] = cross[p][i] - each[i] * weight
                    pivot[own] = jnp.where(inside & (lane > offset + j), 0.0, pivot[own])
                    ahead[p] = [y - weight * v for v, y in zip(pivot, ahead[p])]
        for p in range(problems):
            for t in range(tiles):
                done_ref[t, p * width + base : p * width + after, :] = panel[p][t]
        if not more:
            break
        done, panel = panel, ahead
        if base == LANES // 2 - block:
            defer(0, LANES // 2)
        if base == LANES - 2 * block:
            defer(LANES // 2, LANES - block)
        past = after + block
        stop = LANES if after < LANES else width
        if past >= stop:
            continue
        first = past // LANES
        inverse = ~inside | (lane - offset <= sub)
        below = iota((stop - past, LANES), 1) - offset
        below = (below >= 0) & (below < block)
        for p in range(problems):
            start = p * width
            rows = [parts(x) for x in done[p]]
            left = stack(rows[first : pl.cdiv(stop, LANES)], (0, 0, 1, 1, 0, 2))
            rows[own] = [jnp.where(inverse, x, 0.0) for x in rows[own]]
            update = outer(left, stack(rows, (0, 1, 0, 1, 2, 0)))
            for t in range(tiles):
                old = tile_ref[t, start + past : start + stop, :]
                if t == own:
                    old = jnp.where(below, 0.0, old)
                tile_ref[t, start + past : start + stop, :] = (
                    old
                    - update[past - first * LANES : stop - first * LANES, t * LANES : (t + 1) * LANES]
                )


def unpack(packed, tile_ref, start, width):
    row = iota((LANES, LANES), 0)
    lane = iota((LANES, LANES), 1)
    shared = packed[:LANES, :]
    other = shared.T
    tile_ref[0, start : start + LANES, :] = jnp.where(lane >= row, shared, other)
    tile_ref[0, start + LANES : start + width, :] = jnp.zeros((LANES, LANES), jnp.float32)
    tile_ref[1, start : start + LANES, :] = packed[LANES : 2 * LANES, :]
    diagonal = jnp.broadcast_to(packed[2 * LANES : 2 * LANES + 1, :], (LANES, LANES))
    tile_ref[1, start + LANES : start + width, :] = jnp.where(
        lane < row, shared, jnp.where(lane == row, diagonal, other)
    )


def factors(done_ref, start, width):
    row = iota((width, width), 0)
    lane = iota((width, width), 1)
    whole = jnp.concatenate([done_ref[t, start : start + width, :] for t in range(2)], 1)
    upper = jnp.where(lane > row, whole, jnp.where(lane == row, 1.0 / whole, 0.0))
    return upper, jnp.where(lane <= row, whole, 0.0)


def leaf_kernel(sample_ref, packed_ref, basis_ref, upper_ref, tile_ref, done_ref):
    width = sample_ref.shape[0]
    unpack(packed_ref[...], tile_ref, 0, width)
    eliminate(tile_ref, done_ref, 1, width)
    upper, inverse = factors(done_ref, 0, width)
    upper_ref[...] = upper
    basis_ref[...] = times_transpose(sample_ref[...].T, inverse)


def group_kernel(
    place_ref,
    leaf_ref,
    near_ref,
    far_ref,
    last_ref,
    leaf_upper_ref,
    leaf_transfer_ref,
    pair_transfer_ref,
    group_factor_ref,
    tile_ref,
    done_ref,
    upper_ref,
):
    width = leaf_upper_ref.shape[0]
    pair = leaf_ref[...] + near_ref[...]
    unpack(pair, tile_ref, 0, width)
    unpack(pair + (far_ref[...] + last_ref[...]), tile_ref, width, width)
    eliminate(tile_ref, done_ref, 2, width)
    upper_ref[0], pair_inverse = factors(done_ref, 0, width)
    upper_ref[1], group_inverse = factors(done_ref, width, width)
    leaf_transfer_ref[...] = product_transpose(leaf_upper_ref[...], pair_inverse)
    half = width // 2
    quarter = width // 4
    place = place_ref[0]
    pair_upper = upper_ref[0, pl.ds(pl.multiple_of(place % 2 * half, half), half), :]
    pair_transfer_ref[...] = product_transpose(pair_upper, group_inverse)
    group_factor_ref[...] = upper_ref[
        1, pl.ds(pl.multiple_of(place % 4 * quarter, quarter), quarter), :
    ]


def scratch(problems, width):
    tiles = width // LANES
    return [pltpu.VMEM((tiles, problems * width, LANES), jnp.float32)] * 2


def leaf_factor(sample_t, leaf):
    width, rows = sample_t.shape
    return pl.pallas_call(
        leaf_kernel,
        out_shape=[jax.ShapeDtypeStruct(shape, jnp.float32) for shape in ((rows, width), (width, width))],
        scratch_shapes=scratch(1, width),
        compiler_params=pltpu.CompilerParams(vmem_limit_bytes=24 << 20),
        name="leaf",
    )(sample_t, leaf)


def group_factors(place, leaf, near, far, last, leaf_upper):
    width = leaf_upper.shape[0]
    shapes = [(width, width), (width // 2, width), (width // 4, width)]
    return pl.pallas_call(
        group_kernel,
        out_shape=[jax.ShapeDtypeStruct(shape, jnp.float32) for shape in shapes],
        in_specs=[pl.BlockSpec(memory_space=pltpu.SMEM)]
        + [pl.BlockSpec(memory_space=pltpu.VMEM)] * 5,
        scratch_shapes=scratch(2, width) + [pltpu.VMEM((2, width, width), jnp.float32)],
        compiler_params=pltpu.CompilerParams(vmem_limit_bytes=24 << 20),
        name="group",
    )(place, leaf, near, far, last, leaf_upper)


def local(probes, spectrum):
    devices = lax.axis_size("row") * lax.axis_size("col")
    axes = ("row", "col")
    columns = lax.all_to_all(
        spread(probes, spectrum, devices), axes, split_axis=0, concat_axis=0, tiled=True
    )
    moved = circulant(columns, probes.shape[0], devices)
    sample_t = lax.all_to_all(moved, axes, split_axis=0, concat_axis=0, tiled=True)
    leaf = packed_gram(sample_t)
    far, last, near = (partner(leaf, "col", mask) for mask in (2, 3, 1))
    leaf_basis, leaf_upper = leaf_factor(sample_t, leaf)
    place = lax.axis_index("col").reshape(1).astype(jnp.int32)
    return (leaf_basis, *group_factors(place, leaf, near, far, last, leaf_upper))


def solution(mesh):
    placed = P(("row", "col"), None)
    return jax.shard_map(
        local,
        mesh=mesh,
        in_specs=(placed, placed),
        out_specs=(placed, placed, placed, placed),
        check_vma=False,
    )
```

```python
import math

import jax
import jax.numpy as jnp
import numpy as np
from jax import lax
from jax.experimental import pallas as pl
from jax.experimental.pallas import tpu as pltpu
from jax.sharding import PartitionSpec as P

LANES = 128
HIGHEST = lax.Precision.HIGHEST


def partner(value, axis, mask):
    pairs = [(source, source ^ mask) for source in range(lax.axis_size(axis))]
    return lax.ppermute(value, axis, pairs)


def matmul(left, right):
    return jnp.dot(left, right, precision=HIGHEST, preferred_element_type=jnp.float32)


def circle(product, length):
    angle = 2.0 * np.pi / length * (product % length)
    return np.cos(angle), np.sin(angle)


def halves(table):
    high = table.astype(jnp.bfloat16)
    return np.stack([high, (table - high.astype(np.float64)).astype(jnp.bfloat16)])


def split2(value):
    high = value.astype(jnp.bfloat16)
    return high, (value - high.astype(jnp.float32)).astype(jnp.bfloat16)


def product(left, right):
    def dot(i, j):
        return jnp.dot(left[i], right[j], preferred_element_type=jnp.float32)

    return dot(0, 0) + (dot(0, 1) + dot(1, 0))


def product_transpose(left, right):
    left, right = split2(left), split2(right)

    def dot(i, j):
        return lax.dot_general(
            left[i], right[j], (((1,), (1,)), ((), ())), preferred_element_type=jnp.float32
        )

    return dot(0, 0) + (dot(0, 1) + dot(1, 0))


def tables(devices, split):
    major = devices * split
    total = major * LANES
    order = (np.arange(devices)[None, :] * split + np.arange(split)[:, None]).reshape(-1)
    freq = np.arange(major)
    cos, sin = circle(freq[:, None] * order[None, :], major)
    first = np.block([[cos, sin], [-sin, cos]])
    lane = np.arange(LANES)
    cos, sin = circle(lane[:, None] * lane[None, :], LANES)
    second = np.block([[cos, -sin], [sin, cos]])
    cos_turn, sin_turn = circle(freq[:, None] * lane[None, :], total)
    turn = np.stack([cos_turn, sin_turn])
    return [halves(t) for t in (first, first.T, second, second.T)] + [turn.astype(np.float32)]


def iota(shape, dim):
    return lax.broadcasted_iota(jnp.int32, shape, dim)


def times_transpose(left, right):
    return lax.dot_general(
        left,
        right,
        (((1,), (1,)), ((), ())),
        precision=HIGHEST,
        preferred_element_type=jnp.float32,
    )


def spread_kernel(per_dev, extra):
    def body(probes_ref, spectrum_ref, o_ref):
        rows, width = probes_ref.shape
        split = rows // LANES
        for j in range(split):
            lanes = slice(j * LANES, (j + 1) * LANES)
            o_ref[:, lanes] = probes_ref[lanes, :].T
        place = iota((LANES, rows), 1)
        own = jnp.where(place // split == iota((LANES, rows), 0), spectrum_ref[...], 0.0)
        for t in range(extra):
            part = iota((8, rows), 0) % per_dev + t * per_dev
            pick = jnp.where(iota((8, rows), 1) % split == part, 1.0, 0.0)
            symbol = times_transpose(pick, own)
            for r in range(0, width, 8):
                o_ref[r : r + 8, rows + t * LANES : rows + (t + 1) * LANES] = symbol

    return body


def spread(probes, spectrum, devices):
    rows, width = probes.shape
    per_dev = width // devices
    extra = pl.cdiv(rows // LANES, per_dev)
    return pl.pallas_call(
        spread_kernel(per_dev, extra),
        out_shape=jax.ShapeDtypeStruct((width, rows + extra * LANES), jnp.float32),
        name="spread",
    )(probes, spectrum)


def circulant_kernel(devices, split, per_dev, extra):
    major = devices * split
    pairs = per_dev // 2
    width = devices * per_dev

    def symmetric_symbol(tile_ref):
        lam = jnp.concatenate(
            [
                tile_ref[
                    pl.ds((split + h // per_dev) * width + h % per_dev, devices, stride=per_dev), :
                ]
                for h in range(split)
            ],
            0,
        )
        row = iota((LANES, LANES), 0)
        lane = iota((LANES, LANES), 1)
        flip = jnp.where(row + lane == LANES - 1, 1.0, 0.0)
        head_flip = jnp.where((row + lane) % LANES == 0, 1.0, 0.0)
        back = matmul(lam, jnp.concatenate([flip, head_flip], 1))
        row = iota((major, major), 0)
        lane = iota((major, major), 1)
        turn = jnp.where(row + lane == major, 1.0, 0.0)
        other = jnp.where(
            iota((major, LANES), 0) == 0, back[:, LANES:], matmul(turn, back[:, :LANES])
        )
        return (lam + other) * (0.5 / (major * LANES))

    def body(x_ref, first_ref, first_t_ref, second_ref, second_t_ref, turn_ref, o_ref, tile_ref):
        cos = turn_ref[0]
        sin = turn_ref[1]
        for j in range(split + extra):
            tile_ref[j * width : (j + 1) * width, :] = x_ref[:, j * LANES : (j + 1) * LANES]
        lam = symmetric_symbol(tile_ref)

        def column(c):
            return [
                tile_ref[pl.ds(j * width + c, devices, stride=per_dev), :] for j in range(split)
            ]

        packed = jnp.concatenate(
            [jnp.concatenate(column(2 * q) + column(2 * q + 1), 0) for q in range(pairs)], 1
        )
        mixed = product(first_ref, split2(packed))
        turned = []
        for q in range(pairs):
            real = mixed[:major, q * LANES : (q + 1) * LANES]
            imag = mixed[major:, q * LANES : (q + 1) * LANES]
            turned.append(
                jnp.concatenate([real * cos + imag * sin, imag * cos - real * sin], 1)
            )
        spectra = product(split2(jnp.concatenate(turned, 0)), second_ref)
        lam = jnp.concatenate([lam, lam], 1)
        spectra = jnp.concatenate(
            [spectra[q * major : (q + 1) * major] * lam for q in range(pairs)], 0
        )
        back = product(split2(spectra), second_t_ref)
        turned = []
        for q in range(pairs):
            real = back[q * major : (q + 1) * major, :LANES]
            imag = back[q * major : (q + 1) * major, LANES:]
            turned.append(
                jnp.concatenate([real * cos - imag * sin, imag * cos + real * sin], 0)
            )
        sample = product(first_t_ref, split2(jnp.concatenate(turned, 1)))
        for c in range(per_dev):
            for j in range(split):
                row = (c % 2) * major + j * devices
                lane = (c // 2) * LANES
                tile_ref[pl.ds(j * width + c, devices, stride=per_dev), :] = sample[
                    row : row + devices, lane : lane + LANES
                ]
        for j in range(split):
            o_ref[:, j * LANES : (j + 1) * LANES] = tile_ref[j * width : (j + 1) * width, :]

    return body


def circulant(columns, rows, devices):
    width = columns.shape[0]
    split = rows // LANES
    tiles = columns.shape[1] // LANES
    return pl.pallas_call(
        circulant_kernel(devices, split, width // devices, tiles - split),
        out_shape=jax.ShapeDtypeStruct((width, rows), jnp.float32),
        scratch_shapes=[pltpu.VMEM((tiles * width, LANES), jnp.float32)],
        compiler_params=pltpu.CompilerParams(vmem_limit_bytes=48 << 20),
        name="circulant",
    )(columns, *tables(devices, split))


def packed_gram(sample_t):
    gram = times_transpose(sample_t, sample_t) * (1.0 / sample_t.shape[1])
    row = iota((LANES, LANES), 0)
    lane = iota((LANES, LANES), 1)
    last = gram[LANES:, LANES:]
    shared = jnp.where(lane >= row, gram[:LANES, :LANES], last)
    diagonal = jnp.sum(jnp.where(lane == row, last, 0.0), axis=0, keepdims=True)
    return jnp.concatenate(
        [shared, gram[:LANES, LANES:], jnp.broadcast_to(diagonal, (8, LANES))], 0
    )


def parts(value):
    high = value.astype(jnp.bfloat16).astype(jnp.float32)
    rest = value - high
    middle = rest.astype(jnp.bfloat16).astype(jnp.float32)
    return high, middle, rest - middle


def eliminate(tile_ref, done_ref, problems, width):
    tiles = width // LANES
    block = 8
    shape = (block, LANES)
    sub = iota(shape, 0)
    lane = iota(shape, 1)

    def row_of(value, i):
        return jnp.broadcast_to(value[i : i + 1, :], shape)

    def lane_of(value, l):
        return jnp.broadcast_to(value[:, l : l + 1], shape)

    def turned(value, l):
        only = jnp.sum(jnp.where(lane == sub + l, value, 0.0), axis=1, keepdims=True)
        return jnp.broadcast_to(only, shape)

    def load(base):
        return [
            [
                tile_ref[t, p * width + base : p * width + base + block, :]
                for t in range(tiles)
            ]
            for p in range(problems)
        ]

    def stack(rows, order):
        return jnp.concatenate(
            [jnp.concatenate([row[q] for q in order], 0) for row in rows], 1
        ).astype(jnp.bfloat16)

    def outer(left, right):
        return lax.dot_general(
            left, right, (((0,), (0,)), ((), ())), preferred_element_type=jnp.float32
        )

    def defer(begin, end):
        keep = iota((end - begin, LANES), 1) <= iota((end - begin, LANES), 0) + begin
        for p in range(problems):
            start = p * width
            rows = [parts(done_ref[t, start + begin : start + end, :]) for t in range(tiles)]
            left = stack(rows[1:], (0, 0, 1, 1, 0, 2))
            rows[0] = [jnp.where(keep, x, 0.0) for x in rows[0]]
            update = outer(left, stack(rows, (0, 1, 0, 1, 2, 0)))
            for t in range(tiles):
                tile_ref[t, start + LANES : start + width, :] = (
                    tile_ref[t, start + LANES : start + width, :]
                    - update[:, t * LANES : (t + 1) * LANES]
                )

    panel = load(0)
    for base in range(0, width, block):
        own, offset = divmod(base, LANES)
        after = base + block
        more = after < width
        column = [[lane_of(x[own], offset + l) for l in range(block)] for x in panel]
        inside = (lane >= offset) & (lane < offset + block)
        if more:
            near, shift = divmod(after, LANES)
            cross = [[turned(row_of(x[near], i), shift) for i in range(block)] for x in panel]
            ahead = load(after)
            for x in ahead:
                x[own] = jnp.where(inside, 0.0, x[own])
        for j in range(block):
            hot = (lane == offset + j) & (sub >= j)
            unit = jnp.where(sub == j, 1.0, 0.0)
            for p in range(problems):
                x, c = panel[p], column[p]
                scale = lax.rsqrt(row_of(c[j], j))
                factor = c[j] * scale
                each = {l: row_of(factor, l) for l in range(j + 1, block)}
                for l in range(j + 1, block):
                    c[l] = c[l] - factor * each[l]
                lower = jnp.where(sub > j, factor, 0.0)
                x[own] = jnp.where(hot, unit, x[own])
                pivot = [row_of(y, j) * scale for y in x]
                panel[p] = [
                    jnp.where(sub == j, v, y - lower * v) for v, y in zip(pivot, x)
                ]
                if more:
                    weight = cross[p][j] * scale
                    for i in range(j + 1, block):
                        cross[p][i] = cross[p][i] - each[i] * weight
                    pivot[own] = jnp.where(inside & (lane > offset + j), 0.0, pivot[own])
                    ahead[p] = [y - weight * v for v, y in zip(pivot, ahead[p])]
        for p in range(problems):
            for t in range(tiles):
                done_ref[t, p * width + base : p * width + after, :] = panel[p][t]
        if not more:
            break
        done, panel = panel, ahead
        if base == LANES // 2 - block:
            defer(0, LANES // 2)
        if base == LANES - 2 * block:
            defer(LANES // 2, LANES - block)
        past = after + block
        stop = LANES if after < LANES else width
        if past >= stop:
            continue
        first = past // LANES
        inverse = ~inside | (lane - offset <= sub)
        below = iota((stop - past, LANES), 1) - offset
        below = (below >= 0) & (below < block)
        for p in range(problems):
            start = p * width
            rows = [parts(x) for x in done[p]]
            left = stack(rows[first : pl.cdiv(stop, LANES)], (0, 0, 1, 1, 0, 2))
            rows[own] = [jnp.where(inverse, x, 0.0) for x in rows[own]]
            update = outer(left, stack(rows, (0, 1, 0, 1, 2, 0)))
            for t in range(tiles):
                old = tile_ref[t, start + past : start + stop, :]
                if t == own:
                    old = jnp.where(below, 0.0, old)
                tile_ref[t, start + past : start + stop, :] = (
                    old
                    - update[past - first * LANES : stop - first * LANES, t * LANES : (t + 1) * LANES]
                )


def unpack(packed, tile_ref, start, width):
    row = iota((LANES, LANES), 0)
    lane = iota((LANES, LANES), 1)
    shared = packed[:LANES, :]
    other = shared.T
    tile_ref[0, start : start + LANES, :] = jnp.where(lane >= row, shared, other)
    tile_ref[0, start + LANES : start + width, :] = jnp.zeros((LANES, LANES), jnp.float32)
    tile_ref[1, start : start + LANES, :] = packed[LANES : 2 * LANES, :]
    diagonal = jnp.broadcast_to(packed[2 * LANES : 2 * LANES + 1, :], (LANES, LANES))
    tile_ref[1, start + LANES : start + width, :] = jnp.where(
        lane < row, shared, jnp.where(lane == row, diagonal, other)
    )


def factors(done_ref, start, width):
    row = iota((width, width), 0)
    lane = iota((width, width), 1)
    whole = jnp.concatenate([done_ref[t, start : start + width, :] for t in range(2)], 1)
    upper = jnp.where(lane > row, whole, jnp.where(lane == row, 1.0 / whole, 0.0))
    return upper, jnp.where(lane <= row, whole, 0.0)


def leaf_kernel(sample_ref, packed_ref, basis_ref, upper_ref, tile_ref, done_ref):
    width = sample_ref.shape[0]
    unpack(packed_ref[...], tile_ref, 0, width)
    eliminate(tile_ref, done_ref, 1, width)
    upper, inverse = factors(done_ref, 0, width)
    upper_ref[...] = upper
    basis_ref[...] = times_transpose(sample_ref[...].T, inverse)


def group_kernel(
    place_ref,
    leaf_ref,
    last_ref,
    far_ref,
    near_ref,
    leaf_upper_ref,
    leaf_transfer_ref,
    pair_transfer_ref,
    group_factor_ref,
    tile_ref,
    done_ref,
    upper_ref,
):
    width = leaf_upper_ref.shape[0]
    pair = leaf_ref[...] + near_ref[...]
    unpack(pair, tile_ref, 0, width)
    unpack(pair + (far_ref[...] + last_ref[...]), tile_ref, width, width)
    eliminate(tile_ref, done_ref, 2, width)
    upper_ref[0], pair_inverse = factors(done_ref, 0, width)
    upper_ref[1], group_inverse = factors(done_ref, width, width)
    leaf_transfer_ref[...] = product_transpose(leaf_upper_ref[...], pair_inverse)
    half = width // 2
    quarter = width // 4
    place = place_ref[0]
    pair_upper = upper_ref[0, pl.ds(pl.multiple_of(place % 2 * half, half), half), :]
    pair_transfer_ref[...] = product_transpose(pair_upper, group_inverse)
    group_factor_ref[...] = upper_ref[
        1, pl.ds(pl.multiple_of(place % 4 * quarter, quarter), quarter), :
    ]


def scratch(problems, width):
    tiles = width // LANES
    return [pltpu.VMEM((tiles, problems * width, LANES), jnp.float32)] * 2


def leaf_factor(sample_t, leaf):
    width, rows = sample_t.shape
    return pl.pallas_call(
        leaf_kernel,
        out_shape=[jax.ShapeDtypeStruct(shape, jnp.float32) for shape in ((rows, width), (width, width))],
        scratch_shapes=scratch(1, width),
        compiler_params=pltpu.CompilerParams(vmem_limit_bytes=24 << 20),
        name="leaf",
    )(sample_t, leaf)


def group_factors(place, leaf, near, far, last, leaf_upper):
    width = leaf_upper.shape[0]
    shapes = [(width, width), (width // 2, width), (width // 4, width)]
    return pl.pallas_call(
        group_kernel,
        out_shape=[jax.ShapeDtypeStruct(shape, jnp.float32) for shape in shapes],
        in_specs=[pl.BlockSpec(memory_space=pltpu.SMEM)]
        + [pl.BlockSpec(memory_space=pltpu.VMEM)] * 5,
        scratch_shapes=scratch(2, width) + [pltpu.VMEM((2, width, width), jnp.float32)],
        compiler_params=pltpu.CompilerParams(vmem_limit_bytes=24 << 20),
        name="group",
    )(place, leaf, last, far, near, leaf_upper)


def local(probes, spectrum):
    devices = lax.axis_size("row") * lax.axis_size("col")
    axes = ("row", "col")
    columns = lax.all_to_all(
        spread(probes, spectrum, devices), axes, split_axis=0, concat_axis=0, tiled=True
    )
    moved = circulant(columns, probes.shape[0], devices)
    sample_t = lax.all_to_all(moved, axes, split_axis=0, concat_axis=0, tiled=True)
    leaf = packed_gram(sample_t)
    last, far, near = (partner(leaf, "col", mask) for mask in (3, 2, 1))
    leaf_basis, leaf_upper = leaf_factor(sample_t, leaf)
    place = lax.axis_index("col").reshape(1).astype(jnp.int32)
    return (leaf_basis, *group_factors(place, leaf, near, far, last, leaf_upper))


def solution(mesh):
    placed = P(("row", "col"), None)
    return jax.shard_map(
        local,
        mesh=mesh,
        in_specs=(placed, placed),
        out_specs=(placed, placed, placed, placed),
        check_vma=False,
    )
```
